256 devices in a mesh: lm: 8 (over x, y_hi), tx: 32 (over y_lo, z, core).
Axes of the slice: x: 4, y: 4 (y_hi: 2, y_lo: 2; y = y_hi * 2 + y_lo), z: 8, core: 2. Of those that a mesh axis runs over, the one named last changes fastest.
Arguments:
- features: bfloat16 [65536, 256], P('tx'), may hold values from -1.7265625 to 1.7265625
- landmarks: bfloat16 [8192, 256], P(('lm', 'tx')), may hold values from -1.7265625 to 1.7265625
- whitening: bfloat16 [8192, 64], P(('lm', 'tx')), may hold values from -192 to 192
- cotangent: bfloat16 [65536, 64], P('tx'), may hold values from -6 to 6
Outputs:
- feature_grad: float32 [65536, 256], P(('tx', 'lm'))
- landmark_grad: float32 [8192, 256], P(('lm', 'tx'))
The draws below stay inside these ranges and needn't reach their ends.
All inputs are finite; a program needn't handle non-finite values.
Results may differ from the reference program's by a relative error of at most 0.013.
Values may be sent and summed in bfloat16 or wider, within the bound.
No kernel may reach another device: no remote copies, remote signals or barrier semaphores. Data moves between devices by JAX's collectives and lax.ppermute only.
A program may use at most 64 MiB of HBM per device.

```python
import jax
import jax.numpy as jnp
from jax import lax

F = 256
M = 8192
R = 64
TOK_DEV = 2048
TOKENS = 65536
N_TX = 32


def level_of(own_key, dims, cuts, smallest, top_value):
    def one(position, blocks):
        heights = jax.random.uniform(jax.random.fold_in(jax.random.fold_in(own_key, 6), position), (blocks,), jnp.float32, smallest / len(cuts), top_value / len(cuts))
        return jnp.repeat(jnp.exp(heights), dims[position] // blocks).reshape((-1,) + (1,) * (len(dims) - position - 1))

    level = one(*cuts[0])
    for cut in cuts[1:]:
        level = level * one(*cut)
    return level


def normal_values(rng, dims, spread, bound, cuts=(), kind=jnp.bfloat16):
    entries = jax.random.normal(rng, dims, jnp.float32) * spread
    if len(cuts) > 0:
        entries = level_of(rng, dims, cuts, -0.22, 0.18) * entries
    return jnp.clip(entries, min=-bound, max=bound).astype(kind)


def setup_inputs(seed: int = 0) -> dict:
    streams_of = jax.random.split(jax.random.key(seed), 5)
    features = jnp.clip(jax.random.uniform(streams_of[0], (TOKENS, F), jnp.float32, -1.7265625, 1.7265625) * level_of(streams_of[0], (TOKENS, F), ((0, 32),), -0.4, 0.0), -1.7265625, 1.7265625).astype(jnp.bfloat16)
    landmarks = jnp.clip(jax.random.uniform(streams_of[1], (M, F), jnp.float32, -1.7265625, 1.7265625) * level_of(streams_of[1], (M, F), ((0, 256),), -0.4, 0.0), -1.7265625, 1.7265625).astype(jnp.bfloat16)
    whitening = normal_values(streams_of[2], (M, R), (2981.0 * M ** -0.5), 192.0, ((0, 256),))
    cotangent = normal_values(streams_of[3], (TOKENS, R), 1.0, 6.0, ((0, 32),))
    return {"features": features, "landmarks": landmarks, "whitening": whitening, "cotangent": cotangent}


def reference(features, landmarks, whitening, cotangent):
    gamma = 4.0 / F
    land32 = landmarks.astype(jnp.float32)
    white32 = whitening.astype(jnp.float32)
    sq_land = lax.optimization_barrier(jnp.sum(land32 * land32, axis=1))
    feat_blocks = features.reshape(N_TX, TOK_DEV, F)
    cot_blocks = cotangent.reshape(N_TX, TOK_DEV, R)

    def one_block(carry, inputs):
        feat_block, cot_block = inputs
        feat32 = feat_block.astype(jnp.float32)
        sq_feat = lax.optimization_barrier(jnp.sum(feat32 * feat32, axis=1, keepdims=True))
        cross = jnp.dot(feat32, land32.T, preferred_element_type=jnp.float32)
        kernel = jnp.exp(-gamma * (sq_feat + sq_land[None, :] - 2.0 * cross))
        kernel_b = lax.optimization_barrier(kernel.astype(jnp.bfloat16)).astype(jnp.float32)
        embed = jnp.dot(kernel_b, white32, preferred_element_type=jnp.float32)
        scale = lax.rsqrt(lax.optimization_barrier(jnp.mean(embed * embed, axis=1, keepdims=True)) + 1e-06)
        normed = embed * scale
        cot32 = cot_block.astype(jnp.float32)
        dembed = scale * (cot32 - normed * lax.optimization_barrier(jnp.mean(cot32 * normed, axis=1, keepdims=True)))
        dembed = lax.optimization_barrier(dembed.astype(jnp.bfloat16)).astype(jnp.float32)
        dkernel = jnp.dot(dembed, white32.T, preferred_element_type=jnp.float32)
        coef = lax.optimization_barrier((-gamma * dkernel * kernel).astype(jnp.bfloat16)).astype(jnp.float32)
        row_total = lax.optimization_barrier(jnp.sum(coef, axis=1, keepdims=True))
        col_total = lax.optimization_barrier(jnp.sum(coef, axis=0))
        feat_grad = 2.0 * (row_total * feat32 - jnp.dot(coef, land32, preferred_element_type=jnp.float32))
        land_term = col_total[:, None] * land32 - jnp.dot(coef.T, feat32, preferred_element_type=jnp.float32)
        return (carry + 2.0 * land_term, feat_grad)
    start = jnp.zeros((M, F), jnp.float32)
    land_grad, feat_grads = lax.scan(one_block, start, (feat_blocks, cot_blocks))
    return (feat_grads.reshape(TOKENS, F), land_grad)
```

```python
import jax
import jax.numpy as jnp
from jax import lax
from jax.sharding import Mesh, PartitionSpec as P

LM = ("x", "h")
CHIPS = ("l", "z")
F32 = jnp.float32
BF16 = jnp.bfloat16


def spread(block, axes, size):
    return lax.all_to_all(jnp.broadcast_to(block[None], (size,) + block.shape), axes, 0, 0, tiled=True)


def norm_backward(embed, upstream):
    scale = lax.rsqrt(jnp.mean(embed * embed, axis=1, keepdims=True) + 1e-06)
    normed = embed * scale
    grad = scale * (upstream - normed * jnp.mean(upstream * normed, axis=1, keepdims=True))
    return grad.astype(BF16)


def per_device(features, landmarks, whitening, cotangent):
    toks, width = features.shape
    rank = whitening.shape[1]
    groups = lax.axis_size(LM)
    chips = lax.axis_size(CHIPS)
    rows = landmarks.shape[0]
    group_toks = toks // groups
    gamma = 4.0 / width
    place = lax.axis_index(LM)
    core = lax.axis_index("c")

    both = jnp.concatenate([landmarks, whitening], axis=1)
    both = spread(both, CHIPS, chips).reshape(chips * rows, width + rank)
    both = lax.all_gather(both, "c", axis=0, tiled=True)
    land_rows, white_rows = both[:, :width], both[:, width:]

    feat32 = features.astype(F32)
    land32 = land_rows.astype(F32)
    sq_feat = jnp.sum(feat32 * feat32, axis=1, keepdims=True)
    sq_land = jnp.sum(land32 * land32, axis=1)
    cross = jnp.einsum("nf,mf->nm", features, land_rows, preferred_element_type=F32)
    kernel = jnp.exp(-gamma * (sq_feat + sq_land[None, :] - 2.0 * cross))
    partial_embed = jnp.dot(kernel.astype(BF16), white_rows, preferred_element_type=F32)

    shares = partial_embed.astype(BF16).reshape(groups, group_toks, rank)
    embed = jnp.sum(lax.all_to_all(shares, LM, 0, 0, tiled=True).astype(F32), axis=0)
    own_cot = lax.dynamic_slice_in_dim(cotangent, place * group_toks, group_toks, 0)
    own_dembed = norm_backward(embed, own_cot.astype(F32))
    dembed = spread(own_dembed, LM, groups).reshape(toks, rank)

    dkernel = jnp.einsum("nr,mr->nm", dembed, white_rows, preferred_element_type=F32)
    coef = (-gamma * dkernel * kernel).astype(BF16)
    row_total = jnp.sum(coef, axis=1, keepdims=True, dtype=F32)
    col_total = jnp.sum(coef, axis=0, dtype=F32)

    pulled = jnp.einsum("nm,nf->mf", coef, features, preferred_element_type=F32)
    land_share = (2.0 * (col_total[:, None] * land32 - pulled)).reshape(2, chips, rows, width)
    mine = lax.dynamic_index_in_dim(land_share, core, 0, keepdims=False)
    theirs = lax.dynamic_index_in_dim(land_share, 1 - core, 0, keepdims=False)
    mine = mine + lax.ppermute(theirs.astype(BF16), "c", [(0, 1), (1, 0)]).astype(F32)

    pulled = jnp.dot(coef, land_rows, preferred_element_type=F32)
    feat_share = (2.0 * (row_total * feat32 - pulled)).astype(BF16).reshape(groups, group_toks, width)
    feature_grad = jnp.sum(lax.all_to_all(feat_share, LM, 0, 0, tiled=True).astype(F32), axis=0)

    landmark_grad = jnp.sum(lax.all_to_all(mine.astype(BF16), CHIPS, 0, 0, tiled=True).astype(F32), axis=0)
    return (feature_grad, landmark_grad)


def solution(mesh):
    fine = Mesh(mesh.devices.reshape(4, 2, 2, 8, 2), ("x", "h", "l", "z", "c"))
    tx = ("l", "z", "c")
    placed = (P(tx, None), P(LM + tx, None), P(LM + tx, None), P(tx, None))
    return jax.shard_map(
        per_device,
        mesh=fine,
        in_specs=placed,
        out_specs=(P(tx + LM, None), P(LM + tx, None)),
        check_vma=False,
    )
```

```python
import jax
import jax.numpy as jnp
from jax import lax
from jax.sharding import Mesh, PartitionSpec as P

Y = ("h", "l")
F32 = jnp.float32
BF16 = jnp.bfloat16


def shift(block, axes, step):
    size = lax.axis_size(axes)
    return lax.ppermute(block, axes, [(i, (i + step) % size) for i in range(size)])


def spread(block, axes):
    return [block] + [shift(block, axes, s) for s in range(1, lax.axis_size(axes))]


def collect(pieces, axes, direction):
    total = pieces[0]
    for s in range(1, lax.axis_size(axes)):
        total = total + shift(pieces[s].astype(BF16), axes, direction * s).astype(F32)
    return total


def norm_backward(embed, upstream):
    scale = lax.rsqrt(jnp.mean(embed * embed, axis=1, keepdims=True) + 1e-06)
    normed = embed * scale
    grad = scale * (upstream - normed * jnp.mean(upstream * normed, axis=1, keepdims=True))
    return grad.astype(BF16)


def per_device(features, landmarks, whitening, cotangent):
    toks, width = features.shape
    rank = whitening.shape[1]
    n_x, n_h, n_y, n_z = lax.axis_size("x"), lax.axis_size("h"), lax.axis_size(Y), lax.axis_size("z")
    own = toks // (n_x * n_h)
    rows = landmarks.shape[0]
    gamma = 4.0 / width
    here, half = lax.axis_index("x"), lax.axis_index("h")

    both = jnp.concatenate([landmarks, whitening], axis=1)
    both = jnp.concatenate(spread(both, "z"), axis=0)
    both = jnp.concatenate(spread(both, Y), axis=0)
    both = jnp.concatenate(spread(both, "c"), axis=0)
    land_rows, white_rows = both[:, :width], both[:, width:]

    def taken(array):
        return jnp.concatenate(
            [lax.dynamic_slice_in_dim(array, (((here + s) % n_x) * n_h + half) * own, own, 0) for s in range(n_x)], axis=0
        )

    features, cotangent = taken(features), taken(cotangent)
    feat32 = features.astype(F32)
    land32 = land_rows.astype(F32)
    sq_feat = jnp.sum(feat32 * feat32, axis=1, keepdims=True)
    sq_land = jnp.sum(land32 * land32, axis=1)
    cross = jnp.einsum("nf,mf->nm", features, land_rows, preferred_element_type=F32)
    kernel = jnp.exp(-gamma * (sq_feat + sq_land[None, :] - 2.0 * cross))
    partial_embed = jnp.dot(kernel.astype(BF16), white_rows, preferred_element_type=F32)

    shares = partial_embed.astype(BF16)
    embed = partial_embed
    for s in range(1, n_x):
        embed = embed + jnp.roll(shift(shares, "x", s), -s * own, axis=0).astype(F32)
    dembed = norm_backward(embed, cotangent.astype(F32))

    dkernel = jnp.einsum("nr,mr->nm", dembed, white_rows, preferred_element_type=F32)
    coef = (-gamma * dkernel * kernel).astype(BF16)
    row_total = jnp.sum(coef, axis=1, keepdims=True, dtype=F32)
    col_total = jnp.sum(coef, axis=0, dtype=F32)

    pulled = jnp.einsum("nm,nf->mf", coef, features, preferred_element_type=F32)
    share = (2.0 * (col_total[:, None] * land32 - pulled)).reshape(2, n_y, n_z, rows, width)
    share = collect(share, "c", -1)
    share = collect(share, Y, -1)
    landmark_grad = collect(share, "z", -1)

    pulled = jnp.dot(coef, land_rows, preferred_element_type=F32)
    share = (2.0 * (row_total * feat32 - pulled)).reshape(n_x, own, width)
    feature_grad = collect(share, "x", 1)
    return (feature_grad, landmark_grad)


def solution(mesh):
    fine = Mesh(mesh.devices.reshape(4, 2, 2, 8, 2), ("x", "h", "l", "z", "c"))
    lm, tx = ("x", "h"), ("l", "z", "c")
    placed = (P(tx, None), P(lm + tx, None), P(lm + tx, None), P(tx, None))
    return jax.shard_map(
        per_device,
        mesh=fine,
        in_specs=placed,
        out_specs=(P(tx + lm, None), P(lm + tx, None)),
        check_vma=False,
    )
```

```python
import jax
import jax.numpy as jnp
from jax import lax
from jax.sharding import Mesh, PartitionSpec as P

Y = ("h", "l")
F32 = jnp.float32
BF16 = jnp.bfloat16


def shift(block, axes, step):
    size = lax.axis_size(axes)
    return lax.ppermute(block, axes, [(i, (i + step) % size) for i in range(size)])


def spread(block, axes):
    return [block] + [shift(block, axes, s) for s in range(1, lax.axis_size(axes))]


def collect(pieces, axes, direction):
    total = pieces[0]
    for s in range(1, lax.axis_size(axes)):
        total = total + shift(pieces[s].astype(BF16), axes, direction * s).astype(F32)
    return total


def spread_at_once(block, axes):
    return lax.all_to_all(jnp.broadcast_to(block[None], (lax.axis_size(axes),) + block.shape), axes, 0, 0, tiled=True)


def collect_at_once(pieces, axes):
    return jnp.sum(lax.all_to_all(pieces.astype(BF16), axes, 0, 0, tiled=True).astype(F32), axis=0)


def norm_backward(embed, upstream):
    scale = lax.rsqrt(jnp.mean(embed * embed, axis=1, keepdims=True) + 1e-06)
    normed = embed * scale
    grad = scale * (upstream - normed * jnp.mean(upstream * normed, axis=1, keepdims=True))
    return grad.astype(BF16)


def per_device(features, landmarks, whitening, cotangent):
    toks, width = features.shape
    rank = whitening.shape[1]
    n_x, n_h, n_y, n_z = lax.axis_size("x"), lax.axis_size("h"), lax.axis_size(Y), lax.axis_size("z")
    own = toks // (n_x * n_h)
    rows = landmarks.shape[0]
    gamma = 4.0 / width
    here, half = lax.axis_index("x"), lax.axis_index("h")

    both = jnp.concatenate([landmarks, whitening], axis=1)
    both = spread_at_once(both, "z").reshape(n_z * rows, width + rank)
    both = jnp.concatenate(spread(both, Y), axis=0)
    both = jnp.concatenate(spread(both, "c"), axis=0)
    land_rows, white_rows = both[:, :width], both[:, width:]

    def taken(array):
        return jnp.concatenate(
            [lax.dynamic_slice_in_dim(array, (((here + s) % n_x) * n_h + half) * own, own, 0) for s in range(n_x)], axis=0
        )

    features, cotangent = taken(features), taken(cotangent)
    feat32 = features.astype(F32)
    land32 = land_rows.astype(F32)
    sq_feat = jnp.sum(feat32 * feat32, axis=1, keepdims=True)
    sq_land = jnp.sum(land32 * land32, axis=1)
    cross = jnp.einsum("nf,mf->nm", features, land_rows, preferred_element_type=F32)
    kernel = jnp.exp(-gamma * (sq_feat + sq_land[None, :] - 2.0 * cross))
    partial_embed = jnp.dot(kernel.astype(BF16), white_rows, preferred_element_type=F32)

    shares = partial_embed.astype(BF16)
    embed = partial_embed
    for s in range(1, n_x):
        embed = embed + jnp.roll(shift(shares, "x", s), -s * own, axis=0).astype(F32)
    dembed = norm_backward(embed, cotangent.astype(F32))

    dkernel = jnp.einsum("nr,mr->nm", dembed, white_rows, preferred_element_type=F32)
    coef = (-gamma * dkernel * kernel).astype(BF16)
    row_total = jnp.sum(coef, axis=1, keepdims=True, dtype=F32)
    col_total = jnp.sum(coef, axis=0, dtype=F32)

    pulled = jnp.einsum("nm,nf->mf", coef, features, preferred_element_type=F32)
    share = (2.0 * (col_total[:, None] * land32 - pulled)).reshape(2, n_y, n_z, rows, width)
    share = collect(share, "c", -1)
    share = collect(share, Y, -1)
    landmark_grad = collect_at_once(share, "z")

    pulled = jnp.dot(coef, land_rows, preferred_element_type=F32)
    share = (2.0 * (row_total * feat32 - pulled)).reshape(n_x, own, width)
    feature_grad = collect(share, "x", 1)
    return (feature_grad, landmark_grad)


def solution(mesh):
    fine = Mesh(mesh.devices.reshape(4, 2, 2, 8, 2), ("x", "h", "l", "z", "c"))
    lm, tx = ("x", "h"), ("l", "z", "c")
    placed = (P(tx, None), P(lm + tx, None), P(lm + tx, None), P(tx, None))
    return jax.shard_map(
        per_device,
        mesh=fine,
        in_specs=placed,
        out_specs=(P(tx + lm, None), P(lm + tx, None)),
        check_vma=False,
    )
```

```python
import functools

import jax
import jax.numpy as jnp
from jax import lax
from jax.experimental import pallas as pl
from jax.experimental.pallas import tpu as pltpu
from jax.sharding import Mesh, PartitionSpec as P

Y = ("h", "l")
F32 = jnp.float32
BF16 = jnp.bfloat16
LOG2E = 1.4426950408889634
WHOLE = pl.BlockSpec(memory_space=pltpu.VMEM)
PARAMS = pltpu.CompilerParams(vmem_limit_bytes=20 * 2**20)


def forward_body(count, width, *refs):
    blocks, (feat_t, sq_feat, prior), (kern, embed) = refs[:count], refs[count:-2], refs[-2:]
    rows = blocks[0].shape[0]
    scale = 4.0 / width * LOG2E
    bias = sq_feat[...] * (-scale)
    total = prior[...]
    for i, block in enumerate(blocks):
        land, white = block[:, :width], block[:, width:]
        land32 = land.astype(F32)
        sq_land = jnp.sum(land32 * land32, axis=1, keepdims=True) * (-scale)
        cross = jnp.dot(land, feat_t[...], preferred_element_type=F32)
        value = jnp.exp2(cross * (2.0 * scale) + (bias + sq_land)).astype(BF16)
        kern[i * rows : (i + 1) * rows, :] = value
        total = total + lax.dot_general(white, value, (((0,), (0,)), ((), ())), preferred_element_type=F32)
    embed[...] = total


def forward(blocks, feat_t, sq_feat, prior):
    width, toks = feat_t.shape
    rows = sum(block.shape[0] for block in blocks)
    return pl.pallas_call(
        functools.partial(forward_body, len(blocks), width),
        out_shape=[jax.ShapeDtypeStruct((rows, toks), BF16), jax.ShapeDtypeStruct(prior.shape, F32)],
        in_specs=[WHOLE] * (len(blocks) + 3),
        out_specs=[WHOLE] * 2,
        compiler_params=PARAMS,
    )(*blocks, feat_t, sq_feat, prior)


def backward_body(count, width, *refs):
    blocks, (kern, dembed, feat, prior) = refs[:count], refs[count:-3]
    coef, land_grad, row_total = refs[-3:]
    rows = blocks[0].shape[0]
    total = prior[...]
    for i, block in enumerate(blocks):
        land, white = block[:, :width], block[:, width:]
        at = slice(i * rows, (i + 1) * rows)
        dkernel = jnp.dot(white, dembed[...], preferred_element_type=F32)
        value = (dkernel * kern[at, :].astype(F32)).astype(BF16)
        coef[at, :] = value
        value32 = value.astype(F32)
        total = total + jnp.sum(value32, axis=0, keepdims=True)
        col_total = jnp.sum(value32, axis=1, keepdims=True)
        pulled = jnp.dot(value, feat[...], preferred_element_type=F32)
        land_grad[at, :] = (2.0 * (col_total * land.astype(F32) - pulled)).astype(land_grad.dtype)
    row_total[...] = total


def backward(blocks, kern, dembed, feat, prior, kind):
    toks, width = feat.shape
    rows = kern.shape[0]
    return pl.pallas_call(
        functools.partial(backward_body, len(blocks), width),
        out_shape=[
            jax.ShapeDtypeStruct((rows, toks), BF16),
            jax.ShapeDtypeStruct((rows, width), kind),
            jax.ShapeDtypeStruct(prior.shape, F32),
        ],
        in_specs=[WHOLE] * (len(blocks) + 4),
        out_specs=[WHOLE] * 3,
        compiler_params=PARAMS,
    )(*blocks, kern, dembed, feat, prior)


def feature_body(count, coefs, width, *refs):
    blocks, coef, (feat_t, row_total), outs = refs[:count], refs[count : count + coefs], refs[count + coefs : count + coefs + 2], refs[count + coefs + 2 :]
    rows = blocks[0].shape[0]
    each = count // coefs
    step = feat_t.shape[1] // len(outs)
    pulled = None
    for i, block in enumerate(blocks):
        at = slice(i % each * rows, (i % each + 1) * rows)
        part = lax.dot_general(block[:, :width], coef[i // each][at, :], (((0,), (0,)), ((), ())), preferred_element_type=F32)
        pulled = part if pulled is None else pulled + part
    grad = 2.0 * (row_total[...] * feat_t[...].astype(F32) - pulled)
    for i, out in enumerate(outs):
        out[...] = grad[:, i * step : (i + 1) * step].astype(out.dtype)


def feature_share(blocks, coefs, feat_t, row_total, parts):
    width, toks = feat_t.shape
    kinds = [F32] + [BF16] * (parts - 1)
    return pl.pallas_call(
        functools.partial(feature_body, len(blocks), len(coefs), width),
        out_shape=[jax.ShapeDtypeStruct((width, toks // parts), kind) for kind in kinds],
        in_specs=[WHOLE] * (len(blocks) + len(coefs) + 2),
        out_specs=[WHOLE] * parts,
        compiler_params=PARAMS,
    )(*blocks, *coefs, feat_t, row_total)


def shift(block, axes, step):
    size = lax.axis_size(axes)
    return lax.ppermute(block, axes, [(i, (i + step) % size) for i in range(size)])


def spread(block, axes):
    return [block] + [shift(block, axes, s) for s in range(1, lax.axis_size(axes))]


def collect(pieces, axes, direction):
    total = pieces[0]
    for s in range(1, lax.axis_size(axes)):
        total = total + shift(pieces[s].astype(BF16), axes, direction * s).astype(F32)
    return total


def spread_at_once(block, axes):
    return lax.all_to_all(jnp.broadcast_to(block[None], (lax.axis_size(axes),) + block.shape), axes, 0, 0, tiled=True)


def collect_at_once(pieces, axes):
    return jnp.sum(lax.all_to_all(pieces.astype(BF16), axes, 0, 0, tiled=True).astype(F32), axis=0)


def norm_backward(embed, upstream, factor):
    scale = lax.rsqrt(jnp.mean(embed * embed, axis=0, keepdims=True) + 1e-06)
    normed = embed * scale
    grad = scale * (upstream - normed * jnp.mean(upstream * normed, axis=0, keepdims=True))
    return (factor * grad).astype(BF16)


def per_device(features, landmarks, whitening, cotangent):
    toks, width = features.shape
    rank = whitening.shape[1]
    n_x, n_h, n_y, n_z = lax.axis_size("x"), lax.axis_size("h"), lax.axis_size(Y), lax.axis_size("z")
    own = toks // (n_x * n_h)
    rows = landmarks.shape[0]
    gamma = 4.0 / width
    here, half = lax.axis_index("x"), lax.axis_index("h")

    def taken(array):
        return jnp.concatenate(
            [lax.dynamic_slice_in_dim(array, (((here + s) % n_x) * n_h + half) * own, own, 0) for s in range(n_x)], axis=0
        )

    features, cotangent = taken(features), taken(cotangent)
    feat_t, cot_t = features.T, cotangent.T.astype(F32)
    feat32 = features.astype(F32)
    sq_feat = jnp.sum(feat32 * feat32, axis=1)[None, :]

    both = jnp.concatenate([landmarks, whitening], axis=1)
    both = spread_at_once(both, "z").reshape(n_z * rows, width + rank)
    mine = spread(both, Y)
    theirs = [shift(block, "c", 1) for block in mine]

    kern_mine, embed = forward(mine, feat_t, sq_feat, jnp.zeros((rank, n_x * own), F32))
    kern_theirs, partial_embed = forward(theirs, feat_t, sq_feat, embed)

    shares = partial_embed.astype(BF16)
    embed = partial_embed
    for s in range(1, n_x):
        embed = embed + jnp.roll(shift(shares, "x", s), -s * own, axis=1).astype(F32)
    dembed = norm_backward(embed, cot_t, -gamma)

    no_total = jnp.zeros((1, n_x * own), F32)
    coef_theirs, land_theirs, row_total = backward(theirs, kern_theirs, dembed, features, no_total, BF16)
    coef_mine, land_mine, row_total = backward(mine, kern_mine, dembed, features, row_total, F32)
    share = (land_mine + shift(land_theirs, "c", 1).astype(F32)).reshape(n_y, n_z, rows, width)
    share = collect(share, Y, -1)

    feat_shares = feature_share(mine + theirs, [coef_mine, coef_theirs], feat_t, row_total, n_x)
    landmark_grad = collect_at_once(share, "z")
    feature_grad = collect(feat_shares, "x", 1).T
    return (feature_grad, landmark_grad)


def solution(mesh):
    fine = Mesh(mesh.devices.reshape(4, 2, 2, 8, 2), ("x", "h", "l", "z", "c"))
    lm, tx = ("x", "h"), ("l", "z", "c")
    placed = (P(tx, None), P(lm + tx, None), P(lm + tx, None), P(tx, None))
    return jax.shard_map(
        per_device,
        mesh=fine,
        in_specs=placed,
        out_specs=(P(tx + lm, None), P(lm + tx, None)),
        check_vma=False,
    )
```

```python
import functools

import jax
import jax.numpy as jnp
from jax import lax
from jax.experimental import pallas as pl
from jax.experimental.pallas import tpu as pltpu
from jax.sharding import Mesh, PartitionSpec as P

Y = ("h", "l")
F32 = jnp.float32
BF16 = jnp.bfloat16
LOG2E = 1.4426950408889634
WHOLE = pl.BlockSpec(memory_space=pltpu.VMEM)
PARAMS = pltpu.CompilerParams(vmem_limit_bytes=12 * 2**20)


def call(body, out_shape, *operands):
    return pl.pallas_call(
        body,
        out_shape=out_shape,
        in_specs=[WHOLE] * len(operands),
        out_specs=jax.tree.map(lambda _: WHOLE, out_shape),
        compiler_params=PARAMS,
    )(*operands)


def shaped(shape, kind):
    return jax.ShapeDtypeStruct(shape, kind)


def pack_body(quads, landmarks, whitening, out):
    rows = landmarks.shape[0]
    part = rows // quads
    white = whitening[...].astype(F32)
    white = jnp.concatenate([white[q * part : (q + 1) * part] for q in range(quads)], axis=1).astype(BF16)
    for i in range(out.shape[0]):
        out[i, :rows] = landmarks[...]
        out[i, rows:] = white


def pack(landmarks, whitening, copies):
    rows, width = landmarks.shape
    quads = width // whitening.shape[1]
    return call(functools.partial(pack_body, quads), shaped((copies, rows + rows // quads, width), BF16), landmarks, whitening)


def unpack(block, rank):
    count, packed, width = block.shape
    quads = width // rank
    rows = packed * quads // (quads + 1)
    land = block[:, :rows].reshape(count * rows, width)
    white = block[:, rows:].astype(F32)
    white = jnp.stack([white[:, :, q * rank : (q + 1) * rank] for q in range(quads)], axis=1)
    return land, white.reshape(count * rows, rank).astype(BF16)


def prepare_body(parts, places, features, cot_t, feat, feat_t, sq_feat, cot):
    own = features.shape[0] // parts
    for i, place in enumerate(places()):
        start = pl.multiple_of(place * own, own)
        to = slice(i * own, (i + 1) * own)
        some = features[pl.ds(start, own), :]
        turned = some.T
        turned32 = turned.astype(F32)
        feat[to, :] = some
        feat_t[:, to] = turned
        sq_feat[:, to] = jnp.sum(turned32 * turned32, axis=0, keepdims=True)
        cot[:, to] = cot_t[:, pl.ds(start, own)].astype(F32)


def prepare(features, cot_t, parts, places, count):
    toks, width = features.shape
    toks = toks // parts * count
    rank = cot_t.shape[0]
    shapes = [shaped((toks, width), BF16), shaped((width, toks), BF16), shaped((1, toks), F32), shaped((rank, toks), F32)]
    return call(functools.partial(prepare_body, parts, places), shapes, features, cot_t)


def forward_body(count, rank, first, *refs):
    blocks, (feat_t, sq_feat), (kern, *embeds) = refs[:count], refs[count : count + 2], refs[count + 2 + (not first) :]
    width = feat_t.shape[0]
    scale = 4.0 / width * LOG2E
    bias = sq_feat[...] * (-scale)
    total = None if first else refs[count + 2][...]
    for i, block in enumerate(blocks):
        land, white = unpack(block[...], rank)
        rows = land.shape[0]
        land32 = land.astype(F32)
        sq_land = jnp.sum(land32 * land32, axis=1, keepdims=True) * (-scale)
        cross = jnp.dot(land, feat_t[...], preferred_element_type=F32)
        value = jnp.exp2(cross * (2.0 * scale) + (bias + sq_land)).astype(BF16)
        kern[i * rows : (i + 1) * rows, :] = value
        part = lax.dot_general(white, value, (((0,), (0,)), ((), ())), preferred_element_type=F32)
        total = part if total is None else total + part
    for embed in embeds:
        embed[...] = total.astype(embed.dtype)


def forward(blocks, feat_t, sq_feat, prior, rows, rank):
    toks = feat_t.shape[1]
    shapes = [shaped((rows, toks), BF16), shaped((rank, toks), F32)] + [shaped((rank, toks), BF16)] * len(prior)
    return call(functools.partial(forward_body, len(blocks), rank, not prior), shapes, *blocks, feat_t, sq_feat, *prior)


def norm_body(factor, count, *refs):
    shares, cot, out = refs[:count], refs[count], refs[count + 1]
    own = cot.shape[1] // count
    for p in range(count):
        at = slice(p * own, (p + 1) * own)
        embed = shares[0][:, at]
        for s in range(1, count):
            t = (p + s) % count
            embed = embed + shares[s][:, t * own : (t + 1) * own].astype(F32)
        upstream = cot[:, at]
        scale = lax.rsqrt(jnp.mean(embed * embed, axis=0, keepdims=True) + 1e-06)
        normed = embed * scale
        grad = scale * (upstream - normed * jnp.mean(upstream * normed, axis=0, keepdims=True))
        out[:, at] = (factor * grad).astype(BF16)


def norm_backward(shares, cot, factor):
    return call(functools.partial(norm_body, factor, len(shares)), shaped(cot.shape, BF16), *shares, cot)


def backward_body(count, rank, first, *refs):
    blocks, (kern, dembed, feat) = refs[:count], refs[count : count + 3]
    coef, land_grad, row_total = refs[-3:]
    total = None if first else refs[count + 3][...]
    for i, block in enumerate(blocks):
        land, white = unpack(block[...], rank)
        rows = land.shape[0]
        at = slice(i * rows, (i + 1) * rows)
        dkernel = jnp.dot(white, dembed[...], preferred_element_type=F32)
        value = (dkernel * kern[at, :].astype(F32)).astype(BF16)
        coef[at, :] = value
        value32 = value.astype(F32)
        part = jnp.sum(value32, axis=0, keepdims=True)
        total = part if total is None else total + part
        col_total = jnp.sum(value32, axis=1, keepdims=True)
        pulled = jnp.dot(value, feat[...], preferred_element_type=F32)
        land_grad[at, :] = (2.0 * (col_total * land.astype(F32) - pulled)).astype(land_grad.dtype)
    row_total[...] = total


def backward(blocks, kern, dembed, feat, prior, kind):
    toks, width = feat.shape
    rows = kern.shape[0]
    shapes = [shaped((rows, toks), BF16), shaped((rows, width), kind), shaped((1, toks), F32)]
    body = functools.partial(backward_body, len(blocks), dembed.shape[0], not prior)
    return call(body, shapes, *blocks, kern, dembed, feat, *prior)


def feature_body(count, coefs, rank, *refs):
    blocks, coef, (feat_t, row_total), outs = refs[:count], refs[count : count + coefs], refs[count + coefs : count + coefs + 2], refs[count + coefs + 2 :]
    each = count // coefs
    step = feat_t.shape[1] // len(outs)
    pulled = None
    for i, block in enumerate(blocks):
        land, _ = unpack(block[...], rank)
        rows = land.shape[0]
        at = slice(i % each * rows, (i % each + 1) * rows)
        part = lax.dot_general(land, coef[i // each][at, :], (((0,), (0,)), ((), ())), preferred_element_type=F32)
        pulled = part if pulled is None else pulled + part
    grad = 2.0 * (row_total[...] * feat_t[...].astype(F32) - pulled)
    for i, out in enumerate(outs):
        out[...] = grad[:, i * step : (i + 1) * step].astype(out.dtype)


def feature_share(blocks, coefs, feat_t, row_total, parts, rank):
    width, toks = feat_t.shape
    shapes = [shaped((width, toks // parts), kind) for kind in [F32] + [BF16] * (parts - 1)]
    return call(functools.partial(feature_body, len(blocks), len(coefs), rank), shapes, *blocks, *coefs, feat_t, row_total)


def shift(block, axes, step):
    size = lax.axis_size(axes)
    return lax.ppermute(block, axes, [(i, (i + step) % size) for i in range(size)])


def spread(block, axes):
    return [block] + [shift(block, axes, s) for s in range(1, lax.axis_size(axes))]


def collect(pieces, axes, direction):
    total = pieces[0]
    for s in range(1, lax.axis_size(axes)):
        total = total + shift(pieces[s].astype(BF16), axes, direction * s).astype(F32)
    return total


def collect_at_once(pieces, axes):
    return jnp.sum(lax.all_to_all(pieces.astype(BF16), axes, 0, 0, tiled=True).astype(F32), axis=0)


def per_device(features, landmarks, whitening, cotangent):
    toks, width = features.shape
    rank = whitening.shape[1]
    n_x, n_h, n_y, n_z = lax.axis_size("x"), lax.axis_size("h"), lax.axis_size(Y), lax.axis_size("z")
    rows = landmarks.shape[0]
    gamma = 4.0 / width

    def places():
        here, half = lax.axis_index("x"), lax.axis_index("h")
        return [lax.rem(here + s, n_x) * n_h + half for s in range(n_x)]

    packed = lax.all_to_all(pack(landmarks, whitening, n_z), "z", 0, 0, tiled=True)
    feat, feat_t, sq_feat, cot = prepare(features, cotangent.T, n_x * n_h, places, n_x)
    packed, feat, feat_t, sq_feat, cot = lax.optimization_barrier((packed, feat, feat_t, sq_feat, cot))
    mine = spread(packed, Y)
    theirs = [shift(block, "c", 1) for block in mine]

    half_rows = n_y * n_z * rows
    kern_mine, embed = forward(mine, feat_t, sq_feat, [], half_rows, rank)
    kern_theirs, embed, share = forward(theirs, feat_t, sq_feat, [embed], half_rows, rank)
    dembed = norm_backward([embed] + [shift(share, "x", s) for s in range(1, n_x)], cot, -gamma)

    coef_theirs, land_theirs, row_total = backward(theirs, kern_theirs, dembed, feat, [], BF16)
    coef_mine, land_mine, row_total = backward(mine, kern_mine, dembed, feat, [row_total], F32)
    share = (land_mine + shift(land_theirs, "c", 1).astype(F32)).reshape(n_y, n_z, rows, width)
    share = collect(share, Y, -1)

    feat_shares = feature_share(mine + theirs, [coef_mine, coef_theirs], feat_t, row_total, n_x, rank)
    landmark_grad = collect_at_once(share, "z")
    feature_grad = collect(feat_shares, "x", 1).T
    return (feature_grad, landmark_grad)


def solution(mesh):
    fine = Mesh(mesh.devices.reshape(4, 2, 2, 8, 2), ("x", "h", "l", "z", "c"))
    lm, tx = ("x", "h"), ("l", "z", "c")
    placed = (P(tx, None), P(lm + tx, None), P(lm + tx, None), P(tx, None))
    return jax.shard_map(
        per_device,
        mesh=fine,
        in_specs=placed,
        out_specs=(P(tx + lm, None), P(lm + tx, None)),
        check_vma=False,
    )
```

```python
import functools

import jax
import jax.numpy as jnp
from jax import lax
from jax.experimental import pallas as pl
from jax.experimental.pallas import tpu as pltpu
from jax.sharding import Mesh, PartitionSpec as P

X = ("x",)
Y = ("h", "l")
F32 = jnp.float32
BF16 = jnp.bfloat16
LOG2E = 1.4426950408889634
WHOLE = pl.BlockSpec(memory_space=pltpu.VMEM)
PARAMS = pltpu.CompilerParams(vmem_limit_bytes=12 * 2**20)


def call(body, out_shape, *operands):
    return pl.pallas_call(
        body,
        out_shape=out_shape,
        in_specs=[WHOLE] * len(operands),
        out_specs=jax.tree.map(lambda _: WHOLE, out_shape),
        compiler_params=PARAMS,
    )(*operands)


def shaped(shape, kind):
    return jax.ShapeDtypeStruct(shape, kind)


def pack_body(quads, landmarks, whitening, out):
    rows = landmarks.shape[0]
    part = rows // quads
    white = whitening[...].astype(F32)
    white = jnp.concatenate([white[q * part : (q + 1) * part] for q in range(quads)], axis=1).astype(BF16)
    for i in range(out.shape[0]):
        out[i, :rows] = landmarks[...]
        out[i, rows:] = white


def pack(landmarks, whitening, copies):
    rows, width = landmarks.shape
    quads = width // whitening.shape[1]
    return pl.pallas_call(
        functools.partial(pack_body, quads),
        out_shape=shaped((copies, rows + rows // quads, width), BF16),
        compiler_params=PARAMS,
    )(landmarks, whitening)


def unpack(block, rank):
    count, packed, width = block.shape
    quads = width // rank
    rows = packed * quads // (quads + 1)
    land = block[:, :rows].reshape(count * rows, width)
    white = block[:, rows:].astype(F32)
    white = jnp.stack([white[:, :, q * rank : (q + 1) * rank] for q in range(quads)], axis=1)
    return land, white.reshape(count * rows, rank).astype(BF16)


def prepare_body(parts, places, features, cot_t, feat, feat_t, sq_feat, cot):
    own = features.shape[0] // parts
    for i, place in enumerate(places()):
        start = pl.multiple_of(place * own, own)
        to = slice(i * own, (i + 1) * own)
        some = features[pl.ds(start, own), :]
        turned = some.T
        turned32 = turned.astype(F32)
        feat[to, :] = some
        feat_t[:, to] = turned
        sq_feat[:, to] = jnp.sum(turned32 * turned32, axis=0, keepdims=True)
        cot[:, to] = cot_t[:, pl.ds(start, own)].astype(F32)


def prepare(features, cot_t, parts, places, count):
    toks, width = features.shape
    toks = toks // parts * count
    rank = cot_t.shape[0]
    shapes = [shaped((toks, width), BF16), shaped((width, toks), BF16), shaped((1, toks), F32), shaped((rank, toks), F32)]
    return call(functools.partial(prepare_body, parts, places), shapes, features, cot_t)


def forward_body(count, rank, first, *refs):
    blocks, (feat_t, sq_feat), outs = refs[:count], refs[count : count + 2], refs[count + 2 + (not first) :]
    kerns, embeds = outs[:count], outs[count:]
    width = feat_t.shape[0]
    scale = 4.0 / width * LOG2E
    bias = sq_feat[...] * (-scale)
    total = None if first else refs[count + 2][...]
    for block, kern in zip(blocks, kerns):
        land, white = unpack(block[...], rank)
        land32 = land.astype(F32)
        sq_land = jnp.sum(land32 * land32, axis=1, keepdims=True) * (-scale)
        cross = jnp.dot(land, feat_t[...], preferred_element_type=F32)
        value = jnp.exp2(cross * (2.0 * scale) + (bias + sq_land)).astype(BF16)
        kern[...] = value
        part = lax.dot_general(white, value, (((0,), (0,)), ((), ())), preferred_element_type=F32)
        total = part if total is None else total + part
    for embed in embeds:
        embed[...] = total.astype(embed.dtype)


def forward(blocks, feat_t, sq_feat, prior, rank):
    width, toks = feat_t.shape
    rows = [block.size // (width + rank) for block in blocks]
    shapes = [shaped((n, toks), BF16) for n in rows] + [shaped((rank, toks), F32)] + [shaped((rank, toks), BF16)] * len(prior)
    outs = call(functools.partial(forward_body, len(blocks), rank, not prior), shapes, *blocks, feat_t, sq_feat, *prior)
    return outs[: len(blocks)], outs[len(blocks) :]


def norm_body(factor, count, *refs):
    shares, cot, out = refs[:count], refs[count], refs[count + 1]
    own = cot.shape[1] // count
    for p in range(count):
        at = slice(p * own, (p + 1) * own)
        embed = shares[0][:, at]
        for s in range(1, count):
            t = p ^ s
            embed = embed + shares[s][:, t * own : (t + 1) * own].astype(F32)
        upstream = cot[:, at]
        scale = lax.rsqrt(jnp.mean(embed * embed, axis=0, keepdims=True) + 1e-06)
        normed = embed * scale
        grad = scale * (upstream - normed * jnp.mean(upstream * normed, axis=0, keepdims=True))
        out[:, at] = (factor * grad).astype(BF16)


def norm_backward(shares, cot, factor):
    return call(functools.partial(norm_body, factor, len(shares)), shaped(cot.shape, BF16), *shares, cot)


def backward_body(count, rank, first, *refs):
    blocks, kerns, (dembed, feat) = refs[:count], refs[count : 2 * count], refs[2 * count : 2 * count + 2]
    coef, land_grad, row_total = refs[-3:]
    total = None if first else refs[2 * count + 2][...]
    for i, block in enumerate(blocks):
        land, white = unpack(block[...], rank)
        rows = land.shape[0]
        at = slice(i * rows, (i + 1) * rows)
        dkernel = jnp.dot(white, dembed[...], preferred_element_type=F32)
        value = (dkernel * kerns[i][...].astype(F32)).astype(BF16)
        coef[at, :] = value
        value32 = value.astype(F32)
        part = jnp.sum(value32, axis=0, keepdims=True)
        total = part if total is None else total + part
        col_total = jnp.sum(value32, axis=1, keepdims=True)
        pulled = jnp.dot(value, feat[...], preferred_element_type=F32)
        land_grad[at, :] = (2.0 * (col_total * land.astype(F32) - pulled)).astype(land_grad.dtype)
    row_total[...] = total


def backward(blocks, kerns, dembed, feat, prior, kind):
    toks, width = feat.shape
    rows = sum(kern.shape[0] for kern in kerns)
    shapes = [shaped((rows, toks), BF16), shaped((rows, width), kind), shaped((1, toks), F32)]
    body = functools.partial(backward_body, len(blocks), dembed.shape[0], not prior)
    return call(body, shapes, *blocks, *kerns, dembed, feat, *prior)


def feature_body(count, coefs, rank, *refs):
    blocks, coef, (feat_t, row_total), outs = refs[:count], refs[count : count + coefs], refs[count + coefs : count + coefs + 2], refs[count + coefs + 2 :]
    each = count // coefs
    step = feat_t.shape[1] // len(outs)
    pulled = None
    for i, block in enumerate(blocks):
        land, _ = unpack(block[...], rank)
        rows = land.shape[0]
        at = slice(i % each * rows, (i % each + 1) * rows)
        part = lax.dot_general(land, coef[i // each][at, :], (((0,), (0,)), ((), ())), preferred_element_type=F32)
        pulled = part if pulled is None else pulled + part
    grad = 2.0 * (row_total[...] * feat_t[...].astype(F32) - pulled)
    for i, out in enumerate(outs):
        out[...] = grad[:, i * step : (i + 1) * step].astype(out.dtype)


def feature_share(blocks, coefs, feat_t, row_total, parts, rank):
    width, toks = feat_t.shape
    shapes = [shaped((width, toks // parts), kind) for kind in [F32] * (parts // 2) + [BF16] * (parts // 2)]
    return call(functools.partial(feature_body, len(blocks), len(coefs), rank), shapes, *blocks, *coefs, feat_t, row_total)


def partner(block, ring, which):
    masks = (1, 3)
    perm = [(2 * i + c, 2 * (i ^ masks[which ^ c]) + c) for i in range(lax.axis_size(ring)) for c in range(2)]
    return lax.ppermute(block, ring + ("c",), perm)


def other_core(block):
    return lax.ppermute(block, "c", [(0, 1), (1, 0)])


def spread(block, ring):
    first = partner(block, ring, 0)
    second = partner(block, ring, 1)
    return [block, first, second, partner(first, ring, 1)]


def collect(pieces, ring):
    own, first, second, opposite = pieces
    first = first + partner(opposite.astype(BF16), ring, 1).astype(F32)
    own = own + partner(second.astype(BF16), ring, 1).astype(F32)
    return own + partner(first.astype(BF16), ring, 0).astype(F32)


def collect_at_once(pieces, axes):
    return jnp.sum(lax.all_to_all(pieces.astype(BF16), axes, 0, 0, tiled=True).astype(F32), axis=0)


def per_device(features, landmarks, whitening, cotangent):
    toks, width = features.shape
    rank = whitening.shape[1]
    n_x, n_h, n_y, n_z = lax.axis_size("x"), lax.axis_size("h"), lax.axis_size(Y), lax.axis_size("z")
    rows = landmarks.shape[0]
    gamma = 4.0 / width

    def places():
        here, half, core = lax.axis_index("x"), lax.axis_index("h"), lax.axis_index("c")
        members = [here, here ^ (1 + 2 * core), here ^ (3 - 2 * core), here ^ 2]
        return [member * n_h + half for member in members]

    packed = lax.all_to_all(pack(landmarks, whitening, n_z), "z", 0, 0, tiled=True)
    feat, feat_t, sq_feat, cot = prepare(features, cotangent.T, n_x * n_h, places, n_x)
    packed, feat, feat_t, sq_feat, cot = lax.optimization_barrier((packed, feat, feat_t, sq_feat, cot))
    mine = spread(packed, Y)
    theirs = [other_core(block) for block in mine]

    early, (embed,) = forward(mine[:3] + theirs[:3], feat_t, sq_feat, [], rank)
    late, (embed, share) = forward(mine[3:] + theirs[3:], feat_t, sq_feat, [embed], rank)
    kern_mine, kern_theirs = early[:3] + late[:1], early[3:] + late[1:]
    dembed = norm_backward([embed] + spread(share, X)[1:], cot, -gamma)

    coef_theirs, land_theirs, row_total = backward(theirs, kern_theirs, dembed, feat, [], BF16)
    coef_mine, land_mine, row_total = backward(mine, kern_mine, dembed, feat, [row_total], F32)
    land_share = (land_mine + other_core(land_theirs).astype(F32)).reshape(n_y, n_z, rows, width)
    land_share = collect(land_share, Y)

    feat_shares = feature_share(mine + theirs, [coef_mine, coef_theirs], feat_t, row_total, n_x, rank)
    landmark_grad = collect_at_once(land_share, "z")
    feature_grad = collect(feat_shares, X).T
    return (feature_grad, landmark_grad)


def solution(mesh):
    fine = Mesh(mesh.devices.reshape(4, 2, 2, 8, 2), ("x", "h", "l", "z", "c"))
    lm, tx = ("x", "h"), ("l", "z", "c")
    placed = (P(tx, None), P(lm + tx, None), P(lm + tx, None), P(tx, None))
    return jax.shard_map(
        per_device,
        mesh=fine,
        in_specs=placed,
        out_specs=(P(tx + lm, None), P(lm + tx, None)),
        check_vma=False,
    )
```

```python
import functools

import jax
import jax.numpy as jnp
from jax import lax
from jax.experimental import pallas as pl
from jax.experimental.pallas import tpu as pltpu
from jax.sharding import Mesh, PartitionSpec as P

X = ("x",)
Y = ("h", "l")
F32 = jnp.float32
BF16 = jnp.bfloat16
LOG2E = 1.4426950408889634
WHOLE = pl.BlockSpec(memory_space=pltpu.VMEM)
PARAMS = pltpu.CompilerParams(vmem_limit_bytes=12 * 2**20)


def call(body, out_shape, *operands):
    return pl.pallas_call(
        body,
        out_shape=out_shape,
        in_specs=[WHOLE] * len(operands),
        out_specs=jax.tree.map(lambda _: WHOLE, out_shape),
        compiler_params=PARAMS,
    )(*operands)


def shaped(shape, kind):
    return jax.ShapeDtypeStruct(shape, kind)


def pack_body(quads, landmarks, whitening, out, land, white, sems):
    fetches = [pltpu.make_async_copy(landmarks, land, sems.at[0]), pltpu.make_async_copy(whitening, white, sems.at[1])]
    for fetch in fetches:
        fetch.start()
    for fetch in fetches:
        fetch.wait()
    rows = land.shape[0]
    part = rows // quads
    white32 = white[...].astype(F32)
    beside = jnp.concatenate([white32[q * part : (q + 1) * part] for q in range(quads)], axis=1).astype(BF16)
    for i in range(out.shape[0]):
        out[i, :rows] = land[...]
        out[i, rows:] = beside


def pack(landmarks, whitening, copies):
    rows, width = landmarks.shape
    quads = width // whitening.shape[1]
    return pl.pallas_call(
        functools.partial(pack_body, quads),
        out_shape=shaped((copies, rows + rows // quads, width), BF16),
        in_specs=[pl.BlockSpec(memory_space=pltpu.HBM)] * 2,
        scratch_shapes=[
            pltpu.VMEM(landmarks.shape, BF16),
            pltpu.VMEM(whitening.shape, BF16),
            pltpu.SemaphoreType.DMA((2,)),
        ],
        compiler_params=PARAMS,
    )(*[pltpu.with_memory_space_constraint(array, pltpu.HBM) for array in (landmarks, whitening)])


def unpack(block, rank):
    count, packed, width = block.shape
    quads = width // rank
    rows = packed * quads // (quads + 1)
    land = block[:, :rows].reshape(count * rows, width)
    white = block[:, rows:].astype(F32)
    white = jnp.stack([white[:, :, q * rank : (q + 1) * rank] for q in range(quads)], axis=1)
    return land, white.reshape(count * rows, rank).astype(BF16)


def pieces_of(stacks, count):
    return [stack[i : i + count] for stack in stacks for i in range(0, stack.shape[0], count)]


def prepare_body(parts, places, features, cot_t, feat, feat_t, sq_feat, cot):
    own = features.shape[0] // parts
    for i, place in enumerate(places()):
        start = pl.multiple_of(place * own, own)
        to = slice(i * own, (i + 1) * own)
        some = features[pl.ds(start, own), :]
        turned = some.T
        turned32 = turned.astype(F32)
        feat[to, :] = some
        feat_t[:, to] = turned
        sq_feat[:, to] = jnp.sum(turned32 * turned32, axis=0, keepdims=True)
        cot[:, to] = cot_t[:, pl.ds(start, own)].astype(F32)


def prepare(features, cot_t, parts, places, count):
    toks, width = features.shape
    toks = toks // parts * count
    rank = cot_t.shape[0]
    shapes = [shaped((toks, width), BF16), shaped((width, toks), BF16), shaped((1, toks), F32), shaped((rank, toks), F32)]
    return call(functools.partial(prepare_body, parts, places), shapes, features, cot_t)


def forward_body(count, members, rank, first, *refs):
    blocks, (feat_t, sq_feat), (kern, *embeds) = refs[:count], refs[count : count + 2], refs[count + 2 + (not first) :]
    width = feat_t.shape[0]
    scale = 4.0 / width * LOG2E
    bias = sq_feat[...] * (-scale)
    total = None if first else refs[count + 2][...]
    for i, block in enumerate(pieces_of(blocks, members)):
        land, white = unpack(block, rank)
        rows = land.shape[0]
        land32 = land.astype(F32)
        sq_land = jnp.sum(land32 * land32, axis=1, keepdims=True) * (-scale)
        cross = jnp.dot(land, feat_t[...], preferred_element_type=F32)
        value = jnp.exp2(cross * (2.0 * scale) + (bias + sq_land)).astype(BF16)
        kern[i * rows : (i + 1) * rows, :] = value
        part = lax.dot_general(white, value, (((0,), (0,)), ((), ())), preferred_element_type=F32)
        total = part if total is None else total + part
    for embed in embeds:
        embed[...] = total.astype(embed.dtype)


def forward(blocks, members, feat_t, sq_feat, prior, rows, rank):
    toks = feat_t.shape[1]
    shapes = [shaped((rows, toks), BF16), shaped((rank, toks), F32)] + [shaped((rank, toks), BF16)] * len(prior)
    return call(functools.partial(forward_body, len(blocks), members, rank, not prior), shapes, *blocks, feat_t, sq_feat, *prior)


def moved(ref, place, places, bit):
    own = ref.shape[1] // places
    start = (place ^ bit) * own
    return ref[:, start : start + own].astype(F32)


def pair_sum_body(places, share, other, total, rounded):
    own = share.shape[1] // places
    for p in range(places):
        at = slice(p * own, (p + 1) * own)
        total[:, at] = share[:, at] + moved(other, p, places, 1)
    rounded[...] = total[...].astype(BF16)


def pair_sum(share, other, places):
    shapes = [shaped(share.shape, F32), shaped(share.shape, BF16)]
    return call(functools.partial(pair_sum_body, places), shapes, share, other)


def norm_body(factor, places, share, other, cot, out):
    own = cot.shape[1] // places
    for p in range(places):
        at = slice(p * own, (p + 1) * own)
        embed = share[:, at] + moved(other, p, places, 2)
        upstream = cot[:, at]
        scale = lax.rsqrt(jnp.mean(embed * embed, axis=0, keepdims=True) + 1e-06)
        normed = embed * scale
        grad = scale * (upstream - normed * jnp.mean(upstream * normed, axis=0, keepdims=True))
        out[:, at] = (factor * grad).astype(BF16)


def norm_backward(share, other, cot, factor, places):
    return call(functools.partial(norm_body, factor, places), shaped(cot.shape, BF16), share, other, cot)


def backward_body(count, members, rank, first, *refs):
    blocks, (kern, dembed, feat) = refs[:count], refs[count : count + 3]
    coef, land_grad, row_total = refs[-3:]
    total = None if first else refs[count + 3][...]
    for i, block in enumerate(pieces_of(blocks, members)):
        land, white = unpack(block, rank)
        rows = land.shape[0]
        at = slice(i * rows, (i + 1) * rows)
        dkernel = jnp.dot(white, dembed[...], preferred_element_type=F32)
        value = (dkernel * kern[at, :].astype(F32)).astype(BF16)
        coef[at, :] = value
        value32 = value.astype(F32)
        part = jnp.sum(value32, axis=0, keepdims=True)
        total = part if total is None else total + part
        col_total = jnp.sum(value32, axis=1, keepdims=True)
        pulled = jnp.dot(value, feat[...], preferred_element_type=F32)
        land_grad[at, :] = (2.0 * (col_total * land.astype(F32) - pulled)).astype(land_grad.dtype)
    row_total[...] = total


def backward(blocks, members, kern, dembed, feat, prior, kind):
    toks, width = feat.shape
    rows = kern.shape[0]
    shapes = [shaped((rows, toks), BF16), shaped((rows, width), kind), shaped((1, toks), F32)]
    body = functools.partial(backward_body, len(blocks), members, dembed.shape[0], not prior)
    return call(body, shapes, *blocks, kern, dembed, feat, *prior)


def feature_body(count, members, coefs, rank, *refs):
    blocks, coef, (feat_t, row_total), outs = refs[:count], refs[count : count + coefs], refs[count + coefs : count + coefs + 2], refs[count + coefs + 2 :]
    pieces = pieces_of(blocks, members)
    each = len(pieces) // coefs
    pulled = None
    for i, block in enumerate(pieces):
        land, _ = unpack(block, rank)
        rows = land.shape[0]
        at = slice(i % each * rows, (i % each + 1) * rows)
        part = lax.dot_general(land, coef[i // each][at, :], (((0,), (0,)), ((), ())), preferred_element_type=F32)
        pulled = part if pulled is None else pulled + part
    grad = 2.0 * (row_total[...] * feat_t[...].astype(F32) - pulled)
    start = 0
    for out in outs:
        out[...] = grad[:, start : start + out.shape[1]].astype(out.dtype)
        start += out.shape[1]


def feature_share(blocks, members, coefs, feat_t, row_total, rank):
    width, toks = feat_t.shape
    shapes = [shaped((width, toks // 2), kind) for kind in (F32, BF16)]
    body = functools.partial(feature_body, len(blocks), members, len(coefs), rank)
    return call(body, shapes, *blocks, *coefs, feat_t, row_total)


def shift(block, axes, step):
    size = lax.axis_size(axes)
    return lax.ppermute(block, axes, [(i, (i + step) % size) for i in range(size)])


def partner(block, ring, which):
    masks = (1, 3)
    perm = [(2 * i + c, 2 * (i ^ masks[which ^ c]) + c) for i in range(lax.axis_size(ring)) for c in range(2)]
    return lax.ppermute(block, ring + ("c",), perm)


def spread(block, axes):
    return [block] + [shift(block, axes, s) for s in range(1, lax.axis_size(axes))]


def collect(pieces, axes, direction):
    total = pieces[0]
    for s in range(1, lax.axis_size(axes)):
        total = total + shift(pieces[s].astype(BF16), axes, direction * s).astype(F32)
    return total


def collect_at_once(pieces, axes):
    return jnp.sum(lax.all_to_all(pieces.astype(BF16), axes, 0, 0, tiled=True).astype(F32), axis=0)


def per_device(features, landmarks, whitening, cotangent):
    toks, width = features.shape
    rank = whitening.shape[1]
    n_x, n_h, n_y, n_z = lax.axis_size("x"), lax.axis_size("h"), lax.axis_size(Y), lax.axis_size("z")
    rows = landmarks.shape[0]
    gamma = 4.0 / width

    def places():
        here, half, core = lax.axis_index("x"), lax.axis_index("h"), lax.axis_index("c")
        members = [here, here ^ (1 + 2 * core), here ^ (3 - 2 * core), here ^ 2]
        return [member * n_h + half for member in members]

    packed = lax.all_to_all(pack(landmarks, whitening, n_z), "z", 0, 0, tiled=True)
    feat, feat_t, sq_feat, cot = prepare(features, cotangent.T, n_x * n_h, places, n_x)
    packed, feat, feat_t, sq_feat, cot = lax.optimization_barrier((packed, feat, feat_t, sq_feat, cot))
    mine = spread(packed, Y)
    theirs = [shift(jnp.concatenate(mine, axis=0), "c", 1)]

    half_rows = n_y * n_z * rows
    kern_mine, embed = forward(mine, n_z, feat_t, sq_feat, [], half_rows, rank)
    kern_theirs, embed, share = forward(theirs, n_z, feat_t, sq_feat, [embed], half_rows, rank)
    embed, share = pair_sum(embed, partner(share, X, 0), n_x)
    dembed = norm_backward(embed, partner(share, X, 1), cot, -gamma, n_x)

    coef_theirs, land_theirs, row_total = backward(theirs, n_z, kern_theirs, dembed, feat, [], BF16)
    coef_mine, land_mine, row_total = backward(mine, n_z, kern_mine, dembed, feat, [row_total], F32)
    land_share = (land_mine + shift(land_theirs, "c", 1).astype(F32)).reshape(n_y, n_z, rows, width)
    land_share = collect(land_share, Y, -1)

    near, far = feature_share(mine + theirs, n_z, [coef_mine, coef_theirs], feat_t, row_total, rank)
    land_share, far = lax.optimization_barrier((land_share.astype(BF16), partner(far, X, 1)))
    landmark_grad = collect_at_once(land_share, "z")
    near = near + far.astype(F32)
    own = near.shape[1] // 2
    feature_grad = (near[:, :own] + partner(near[:, own:].astype(BF16), X, 0).astype(F32)).T
    return (feature_grad, landmark_grad)


def solution(mesh):
    fine = Mesh(mesh.devices.reshape(4, 2, 2, 8, 2), ("x", "h", "l", "z", "c"))
    lm, tx = ("x", "h"), ("l", "z", "c")
    placed = (P(tx, None), P(lm + tx, None), P(lm + tx, None), P(tx, None))
    return jax.shard_map(
        per_device,
        mesh=fine,
        in_specs=placed,
        out_specs=(P(tx + lm, None), P(lm + tx, None)),
        check_vma=False,
    )
```

```python
import functools

import jax
import jax.numpy as jnp
from jax import lax
from jax.experimental import pallas as pl
from jax.experimental.pallas import tpu as pltpu
from jax.sharding import Mesh, PartitionSpec as P

X = ("x",)
Y = ("h", "l")
F32 = jnp.float32
BF16 = jnp.bfloat16
LOG2E = 1.4426950408889634
WHOLE = pl.BlockSpec(memory_space=pltpu.VMEM)
PARAMS = pltpu.CompilerParams(vmem_limit_bytes=12 * 2**20)


def call(body, out_shape, *operands):
    return pl.pallas_call(
        body,
        out_shape=out_shape,
        in_specs=[WHOLE] * len(operands),
        out_specs=jax.tree.map(lambda _: WHOLE, out_shape),
        compiler_params=PARAMS,
    )(*operands)


def shaped(shape, kind):
    return jax.ShapeDtypeStruct(shape, kind)


def pack_body(quads, landmarks, whitening, out, land, white, sems):
    fetches = [pltpu.make_async_copy(landmarks, land, sems.at[0]), pltpu.make_async_copy(whitening, white, sems.at[1])]
    for fetch in fetches:
        fetch.start()
    for fetch in fetches:
        fetch.wait()
    rows = land.shape[0]
    part = rows // quads
    white32 = white[...].astype(F32)
    beside = jnp.concatenate([white32[q * part : (q + 1) * part] for q in range(quads)], axis=1).astype(BF16)
    for i in range(out.shape[0]):
        out[i, :rows] = land[...]
        out[i, rows:] = beside


def pack(landmarks, whitening, copies):
    rows, width = landmarks.shape
    quads = width // whitening.shape[1]
    return pl.pallas_call(
        functools.partial(pack_body, quads),
        out_shape=shaped((copies, rows + rows // quads, width), BF16),
        in_specs=[pl.BlockSpec(memory_space=pltpu.HBM)] * 2,
        scratch_shapes=[
            pltpu.VMEM(landmarks.shape, BF16),
            pltpu.VMEM(whitening.shape, BF16),
            pltpu.SemaphoreType.DMA((2,)),
        ],
        compiler_params=PARAMS,
    )(*[pltpu.with_memory_space_constraint(array, pltpu.HBM) for array in (landmarks, whitening)])


def unpack(block, rank):
    count, packed, width = block.shape
    quads = width // rank
    rows = packed * quads // (quads + 1)
    land = block[:, :rows].reshape(count * rows, width)
    white = block[:, rows:].astype(F32)
    white = jnp.stack([white[:, :, q * rank : (q + 1) * rank] for q in range(quads)], axis=1)
    return land, white.reshape(count * rows, rank).astype(BF16)


def pieces_of(stacks, count):
    return [stack[i : i + count] for stack in stacks for i in range(0, stack.shape[0], count)]


def prepare_body(parts, places, features, cot_t, feat, feat_t, sq_feat, cot):
    own = features.shape[0] // parts
    for i, place in enumerate(places()):
        start = pl.multiple_of(place * own, own)
        to = slice(i * own, (i + 1) * own)
        some = features[pl.ds(start, own), :]
        turned = some.T
        turned32 = turned.astype(F32)
        feat[to, :] = some
        feat_t[:, to] = turned
        sq_feat[:, to] = jnp.sum(turned32 * turned32, axis=0, keepdims=True)
        cot[:, to] = cot_t[:, pl.ds(start, own)].astype(F32)


def prepare(features, cot_t, parts, places, count):
    toks, width = features.shape
    toks = toks // parts * count
    rank = cot_t.shape[0]
    shapes = [shaped((toks, width), BF16), shaped((width, toks), BF16), shaped((1, toks), F32), shaped((rank, toks), F32)]
    return call(functools.partial(prepare_body, parts, places), shapes, features, cot_t)


def forward_body(count, members, rank, first, *refs):
    blocks, (feat_t, sq_feat), (kern, *embeds) = refs[:count], refs[count : count + 2], refs[count + 2 + (not first) :]
    width = feat_t.shape[0]
    scale = 4.0 / width * LOG2E
    bias = sq_feat[...] * (-scale)
    total = None if first else refs[count + 2][...]
    for i, block in enumerate(pieces_of(blocks, members)):
        land, white = unpack(block, rank)
        rows = land.shape[0]
        land32 = land.astype(F32)
        sq_land = jnp.sum(land32 * land32, axis=1, keepdims=True) * (-scale)
        cross = jnp.dot(land, feat_t[...], preferred_element_type=F32)
        value = jnp.exp2(cross * (2.0 * scale) + (bias + sq_land)).astype(BF16)
        kern[i * rows : (i + 1) * rows, :] = value
        part = lax.dot_general(white, value, (((0,), (0,)), ((), ())), preferred_element_type=F32)
        total = part if total is None else total + part
    for embed in embeds:
        embed[...] = total.astype(embed.dtype)


def forward(blocks, members, feat_t, sq_feat, prior, rows, rank):
    toks = feat_t.shape[1]
    shapes = [shaped((rows, toks), BF16), shaped((rank, toks), BF16 if prior else F32)]
    return call(functools.partial(forward_body, len(blocks), members, rank, not prior), shapes, *blocks, feat_t, sq_feat, *prior)


def norm_body(factor, shares, cot, out):
    places = shares.shape[0]
    embed = shares[0].astype(F32)
    for s in range(1, places):
        embed = embed + shares[s].astype(F32)
    upstream = cot[...]
    scale = lax.rsqrt(jnp.mean(embed * embed, axis=0, keepdims=True) + 1e-06)
    normed = embed * scale
    grad = scale * (upstream - normed * jnp.mean(upstream * normed, axis=0, keepdims=True))
    out[...] = (factor * grad).astype(BF16)


def norm_backward(shares, cot, factor):
    return call(functools.partial(norm_body, factor), shaped(cot.shape, BF16), shares, cot)


def backward_body(count, members, rank, first, *refs):
    blocks, (kern, dembed, feat) = refs[:count], refs[count : count + 3]
    coef, land_grad, row_total = refs[-3:]
    total = None if first else refs[count + 3][...]
    for i, block in enumerate(pieces_of(blocks, members)):
        land, white = unpack(block, rank)
        rows = land.shape[0]
        at = slice(i * rows, (i + 1) * rows)
        dkernel = jnp.dot(white, dembed[...], preferred_element_type=F32)
        value = (dkernel * kern[at, :].astype(F32)).astype(BF16)
        coef[at, :] = value
        value32 = value.astype(F32)
        part = jnp.sum(value32, axis=0, keepdims=True)
        total = part if total is None else total + part
        col_total = jnp.sum(value32, axis=1, keepdims=True)
        pulled = jnp.dot(value, feat[...], preferred_element_type=F32)
        land_grad[at, :] = (2.0 * (col_total * land.astype(F32) - pulled)).astype(land_grad.dtype)
    row_total[...] = total


def backward(blocks, members, kern, dembed, feat, prior, kind):
    toks, width = feat.shape
    rows = kern.shape[0]
    shapes = [shaped((rows, toks), BF16), shaped((rows, width), kind), shaped((1, toks), F32)]
    body = functools.partial(backward_body, len(blocks), members, dembed.shape[0], not prior)
    return call(body, shapes, *blocks, kern, dembed, feat, *prior)


def feature_body(count, members, coefs, rank, *refs):
    blocks, coef, (feat_t, row_total), outs = refs[:count], refs[count : count + coefs], refs[count + coefs : count + coefs + 2], refs[-1]
    pieces = pieces_of(blocks, members)
    each = len(pieces) // coefs
    pulled = None
    for i, block in enumerate(pieces):
        land, _ = unpack(block, rank)
        rows = land.shape[0]
        at = slice(i % each * rows, (i % each + 1) * rows)
        part = lax.dot_general(land, coef[i // each][at, :], (((0,), (0,)), ((), ())), preferred_element_type=F32)
        pulled = part if pulled is None else pulled + part
    grad = 2.0 * (row_total[...] * feat_t[...].astype(F32) - pulled)
    groups, _, own = outs.shape
    for i in range(groups):
        outs[i] = grad[:, i * own : (i + 1) * own].astype(BF16)


def feature_share(blocks, members, coefs, feat_t, row_total, rank, groups):
    width, toks = feat_t.shape
    shapes = shaped((groups, width, toks // groups), BF16)
    body = functools.partial(feature_body, len(blocks), members, len(coefs), rank)
    return call(body, shapes, *blocks, *coefs, feat_t, row_total)


def shift(block, axes, step):
    size = lax.axis_size(axes)
    return lax.ppermute(block, axes, [(i, (i + step) % size) for i in range(size)])


def collect_at_once(pieces, axes):
    return jnp.sum(lax.all_to_all(pieces.astype(BF16), axes, 0, 0, tiled=True).astype(F32), axis=0)


def per_device(features, landmarks, whitening, cotangent):
    toks, width = features.shape
    rank = whitening.shape[1]
    n_x, n_h, n_y, n_z = lax.axis_size("x"), lax.axis_size("h"), lax.axis_size(Y), lax.axis_size("z")
    rows = landmarks.shape[0]
    gamma = 4.0 / width

    def places():
        return [s * n_h + lax.axis_index("h") for s in range(n_x)]

    packed = lax.all_to_all(pack(landmarks, whitening, n_y * n_z), Y + ("z",), 0, 0, tiled=True)
    feat, feat_t, sq_feat, cot = prepare(features, cotangent.T, n_x * n_h, places, n_x)
    packed, feat, feat_t, sq_feat, cot = lax.optimization_barrier((packed, feat, feat_t, sq_feat, cot))
    mine, theirs = [packed], [shift(packed, "c", 1)]

    half_rows = n_y * n_z * rows
    kern_mine, embed = forward(mine, n_z, feat_t, sq_feat, [], half_rows, rank)
    kern_theirs, share = forward(theirs, n_z, feat_t, sq_feat, [embed], half_rows, rank)
    shares = lax.all_to_all(jnp.broadcast_to(share[None], (n_x,) + share.shape), "x", 0, 0, tiled=True)
    dembed = norm_backward(shares, cot, -gamma)

    coef_theirs, land_theirs, row_total = backward(theirs, n_z, kern_theirs, dembed, feat, [], BF16)
    coef_mine, land_mine, row_total = backward(mine, n_z, kern_mine, dembed, feat, [row_total], F32)
    land_share = (land_mine + shift(land_theirs, "c", 1).astype(F32)).reshape(n_y, n_z, rows, width)
    land_share = collect_at_once(land_share, Y)

    feat_share = feature_share(mine + theirs, n_z, [coef_mine, coef_theirs], feat_t, row_total, rank, n_x)
    landmark_grad = collect_at_once(land_share, "z")
    feature_grad = collect_at_once(feat_share, "x").T
    return (feature_grad, landmark_grad)


def solution(mesh):
    fine = Mesh(mesh.devices.reshape(4, 2, 2, 8, 2), ("x", "h", "l", "z", "c"))
    lm, tx = ("x", "h"), ("l", "z", "c")
    placed = (P(tx, None), P(lm + tx, None), P(lm + tx, None), P(tx, None))
    return jax.shard_map(
        per_device,
        mesh=fine,
        in_specs=placed,
        out_specs=(P(tx + lm, None), P(lm + tx, None)),
        check_vma=False,
    )
```

```python
import functools

import jax
import jax.numpy as jnp
from jax import lax
from jax.experimental import pallas as pl
from jax.experimental.pallas import tpu as pltpu
from jax.sharding import Mesh, PartitionSpec as P

X = ("x",)
Y = ("h", "l")
F32 = jnp.float32
BF16 = jnp.bfloat16
LOG2E = 1.4426950408889634
WHOLE = pl.BlockSpec(memory_space=pltpu.VMEM)
PARAMS = pltpu.CompilerParams(vmem_limit_bytes=12 * 2**20)


def call(body, out_shape, *operands):
    return pl.pallas_call(
        body,
        out_shape=out_shape,
        in_specs=[WHOLE] * len(operands),
        out_specs=jax.tree.map(lambda _: WHOLE, out_shape),
        compiler_params=PARAMS,
    )(*operands)


def shaped(shape, kind):
    return jax.ShapeDtypeStruct(shape, kind)


def pack_body(quads, landmarks, whitening, out, land, white, sems):
    fetches = [pltpu.make_async_copy(landmarks, land, sems.at[0]), pltpu.make_async_copy(whitening, white, sems.at[1])]
    for fetch in fetches:
        fetch.start()
    for fetch in fetches:
        fetch.wait()
    rows = land.shape[0]
    part = rows // quads
    white32 = white[...].astype(F32)
    beside = jnp.concatenate([white32[q * part : (q + 1) * part] for q in range(quads)], axis=1).astype(BF16)
    for i in range(out.shape[0]):
        out[i, :rows] = land[...]
        out[i, rows:] = beside


def pack(landmarks, whitening, copies):
    rows, width = landmarks.shape
    quads = width // whitening.shape[1]
    return pl.pallas_call(
        functools.partial(pack_body, quads),
        out_shape=shaped((copies, rows + rows // quads, width), BF16),
        in_specs=[pl.BlockSpec(memory_space=pltpu.HBM)] * 2,
        scratch_shapes=[
            pltpu.VMEM(landmarks.shape, BF16),
            pltpu.VMEM(whitening.shape, BF16),
            pltpu.SemaphoreType.DMA((2,)),
        ],
        compiler_params=PARAMS,
    )(*[pltpu.with_memory_space_constraint(array, pltpu.HBM) for array in (landmarks, whitening)])


def unpack(block, rank):
    count, packed, width = block.shape
    quads = width // rank
    rows = packed * quads // (quads + 1)
    land = block[:, :rows].reshape(count * rows, width)
    white = block[:, rows:].astype(F32)
    white = jnp.stack([white[:, :, q * rank : (q + 1) * rank] for q in range(quads)], axis=1)
    return land, white.reshape(count * rows, rank).astype(BF16)


def prepare_body(parts, places, features, cot_t, feat, feat_t, sq_feat, cot):
    own = features.shape[0] // parts
    for i, place in enumerate(places()):
        start = pl.multiple_of(place * own, own)
        to = slice(i * own, (i + 1) * own)
        some = features[pl.ds(start, own), :]
        turned = some.T
        turned32 = turned.astype(F32)
        feat[to, :] = some
        feat_t[:, to] = turned
        sq_feat[:, to] = jnp.sum(turned32 * turned32, axis=0, keepdims=True)
        cot[:, to] = cot_t[:, pl.ds(start, own)].astype(F32)


def prepare(features, cot_t, parts, places, count):
    toks, width = features.shape
    toks = toks // parts * count
    rank = cot_t.shape[0]
    shapes = [shaped((toks, width), BF16), shaped((width, toks), BF16), shaped((1, toks), F32), shaped((rank, toks), F32)]
    return call(functools.partial(prepare_body, parts, places), shapes, features, cot_t)


def forward_body(count, rank, first, *refs):
    blocks, (feat_t, sq_feat), outs = refs[:count], refs[count : count + 2], refs[count + 2 + (not first) :]
    kerns, embeds = outs[:count], outs[count:]
    width = feat_t.shape[0]
    scale = 4.0 / width * LOG2E
    bias = sq_feat[...] * (-scale)
    total = None if first else refs[count + 2][...]
    for block, kern in zip(blocks, kerns):
        land, white = unpack(block[...], rank)
        land32 = land.astype(F32)
        sq_land = jnp.sum(land32 * land32, axis=1, keepdims=True) * (-scale)
        cross = jnp.dot(land, feat_t[...], preferred_element_type=F32)
        value = jnp.exp2(cross * (2.0 * scale) + (bias + sq_land)).astype(BF16)
        kern[...] = value
        part = lax.dot_general(white, value, (((0,), (0,)), ((), ())), preferred_element_type=F32)
        total = part if total is None else total + part
    for embed in embeds:
        embed[...] = total.astype(embed.dtype)


def forward(blocks, feat_t, sq_feat, prior, last, rank):
    width, toks = feat_t.shape
    shapes = [shaped((block.size // (width + rank), toks), BF16) for block in blocks]
    shapes += [shaped((rank, toks), kind) for kind in ([F32, BF16] if last else [F32])]
    outs = call(functools.partial(forward_body, len(blocks), rank, not prior), shapes, *blocks, feat_t, sq_feat, *prior)
    return outs[: len(blocks)], outs[len(blocks) :]


def moved(ref, place, places, bit):
    own = ref.shape[1] // places
    start = (place ^ bit) * own
    return ref[:, start : start + own].astype(F32)


def pair_sum_body(places, share, other, total, rounded):
    own = share.shape[1] // places
    for p in range(places):
        at = slice(p * own, (p + 1) * own)
        total[:, at] = share[:, at] + moved(other, p, places, 1)
    rounded[...] = total[...].astype(BF16)


def pair_sum(share, other, places):
    shapes = [shaped(share.shape, F32), shaped(share.shape, BF16)]
    return call(functools.partial(pair_sum_body, places), shapes, share, other)


def norm_body(factor, places, share, other, cot, out):
    own = cot.shape[1] // places
    for p in range(places):
        at = slice(p * own, (p + 1) * own)
        embed = share[:, at] + moved(other, p, places, 2)
        upstream = cot[:, at]
        scale = lax.rsqrt(jnp.mean(embed * embed, axis=0, keepdims=True) + 1e-06)
        normed = embed * scale
        grad = scale * (upstream - normed * jnp.mean(upstream * normed, axis=0, keepdims=True))
        out[:, at] = (factor * grad).astype(BF16)


def norm_backward(share, other, cot, factor, places):
    return call(functools.partial(norm_body, factor, places), shaped(cot.shape, BF16), share, other, cot)


def backward_body(count, rank, first, *refs):
    blocks, kerns, (dembed, feat) = refs[:count], refs[count : 2 * count], refs[2 * count : 2 * count + 2]
    coef, land_grad, row_total = refs[-3:]
    total = None if first else refs[2 * count + 2][...]
    for i, block in enumerate(blocks):
        land, white = unpack(block[...], rank)
        rows = land.shape[0]
        at = slice(i * rows, (i + 1) * rows)
        dkernel = jnp.dot(white, dembed[...], preferred_element_type=F32)
        value = (dkernel * kerns[i][...].astype(F32)).astype(BF16)
        coef[at, :] = value
        value32 = value.astype(F32)
        part = jnp.sum(value32, axis=0, keepdims=True)
        total = part if total is None else total + part
        col_total = jnp.sum(value32, axis=1, keepdims=True)
        pulled = jnp.dot(value, feat[...], preferred_element_type=F32)
        land_grad[at, :] = (2.0 * (col_total * land.astype(F32) - pulled)).astype(land_grad.dtype)
    row_total[...] = total


def backward(blocks, kerns, dembed, feat, prior, kind):
    toks, width = feat.shape
    rows = sum(kern.shape[0] for kern in kerns)
    shapes = [shaped((rows, toks), BF16), shaped((rows, width), kind), shaped((1, toks), F32)]
    body = functools.partial(backward_body, len(blocks), dembed.shape[0], not prior)
    return call(body, shapes, *blocks, *kerns, dembed, feat, *prior)


def feature_body(count, coefs, rank, *refs):
    blocks, coef, (feat_t, row_total), outs = refs[:count], refs[count : count + coefs], refs[count + coefs : count + coefs + 2], refs[count + coefs + 2 :]
    each = count // coefs
    pulled = None
    for i, block in enumerate(blocks):
        land, _ = unpack(block[...], rank)
        rows = land.shape[0]
        at = slice(i % each * rows, (i % each + 1) * rows)
        part = lax.dot_general(land, coef[i // each][at, :], (((0,), (0,)), ((), ())), preferred_element_type=F32)
        pulled = part if pulled is None else pulled + part
    grad = 2.0 * (row_total[...] * feat_t[...].astype(F32) - pulled)
    start = 0
    for out in outs:
        out[...] = grad[:, start : start + out.shape[1]].astype(out.dtype)
        start += out.shape[1]


def feature_share(blocks, coefs, feat_t, row_total, parts, rank):
    width, toks = feat_t.shape
    shapes = [shaped((width, toks // parts), kind) for kind in [F32] + [BF16] * (parts - 1)]
    body = functools.partial(feature_body, len(blocks), len(coefs), rank)
    return call(body, shapes, *blocks, *coefs, feat_t, row_total)


def shift(block, axes, step):
    size = lax.axis_size(axes)
    return lax.ppermute(block, axes, [(i, (i + step) % size) for i in range(size)])


def partner(block, ring, which):
    masks = (1, 3)
    perm = [(2 * i + c, 2 * (i ^ masks[which ^ c]) + c) for i in range(lax.axis_size(ring)) for c in range(2)]
    return lax.ppermute(block, ring + ("c",), perm)


def spread(block, axes):
    return [block] + [shift(block, axes, s) for s in range(1, lax.axis_size(axes))]


def collect(pieces, axes, direction):
    total = pieces[0]
    for s in range(1, lax.axis_size(axes)):
        total = total + shift(pieces[s].astype(BF16), axes, direction * s).astype(F32)
    return total


def collect_at_once(pieces, axes):
    return jnp.sum(lax.all_to_all(pieces.astype(BF16), axes, 0, 0, tiled=True).astype(F32), axis=0)


def per_device(features, landmarks, whitening, cotangent):
    toks, width = features.shape
    rank = whitening.shape[1]
    n_x, n_h, n_y, n_z = lax.axis_size("x"), lax.axis_size("h"), lax.axis_size(Y), lax.axis_size("z")
    rows = landmarks.shape[0]
    gamma = 4.0 / width

    def places():
        here, half, core = lax.axis_index("x"), lax.axis_index("h"), lax.axis_index("c")
        members = [here, here ^ (1 + 2 * core), here ^ (3 - 2 * core), here ^ 2]
        return [member * n_h + half for member in members]

    packed = lax.all_to_all(pack(landmarks, whitening, n_z), "z", 0, 0, tiled=True)
    feat, feat_t, sq_feat, cot = prepare(features, cotangent.T, n_x * n_h, places, n_x)
    packed, feat, feat_t, sq_feat, cot = lax.optimization_barrier((packed, feat, feat_t, sq_feat, cot))
    mine = spread(packed, Y)
    theirs = [shift(packed, "c", 1)] + [None] * (n_y - 1)

    order = (0, 3, 1, 2)
    kern_mine, kern_theirs = {}, {}
    embed = []
    for step in range(n_y + 1):
        todo = [(kern_theirs, theirs, order[step - 1])] * (step > 0) + [(kern_mine, mine, order[step % n_y])] * (step < n_y)
        kerns, embed = forward([blocks[s] for _, blocks, s in todo], feat_t, sq_feat, embed, step == n_y, rank)
        for (where, _, s), kern in zip(todo, kerns):
            where[s] = kern
        if step + 1 < n_y:
            s = order[step + 1]
            mine[s], embed = lax.optimization_barrier((mine[s], embed))
            theirs[s] = shift(mine[s], "c", 1)
    kern_mine, kern_theirs = [kern_mine[s] for s in range(n_y)], [kern_theirs[s] for s in range(n_y)]
    embed, share = embed
    embed, share = pair_sum(embed, partner(share, X, 0), n_x)
    dembed = norm_backward(embed, partner(share, X, 1), cot, -gamma, n_x)

    coef_theirs, land_theirs, row_total = backward(theirs, kern_theirs, dembed, feat, [], BF16)
    coef_mine, land_mine, row_total = backward(mine, kern_mine, dembed, feat, [row_total], F32)
    land_share = (land_mine + shift(land_theirs, "c", 1).astype(F32)).reshape(n_y, n_z, rows, width)
    land_share = collect(land_share, Y, -1)

    own, first, second, opposite = feature_share(mine + theirs, [coef_mine, coef_theirs], feat_t, row_total, n_x, rank)
    landmark_grad = collect_at_once(land_share, "z")
    arrived = [partner(first, X, 0), partner(second, X, 1), shift(opposite, "x", 2)]
    feature_grad = (own + sum(share.astype(F32) for share in arrived)).T
    return (feature_grad, landmark_grad)


def solution(mesh):
    fine = Mesh(mesh.devices.reshape(4, 2, 2, 8, 2), ("x", "h", "l", "z", "c"))
    lm, tx = ("x", "h"), ("l", "z", "c")
    placed = (P(tx, None), P(lm + tx, None), P(lm + tx, None), P(tx, None))
    return jax.shard_map(
        per_device,
        mesh=fine,
        in_specs=placed,
        out_specs=(P(tx + lm, None), P(lm + tx, None)),
        check_vma=False,
    )
```

```python
import functools

import jax
import jax.numpy as jnp
from jax import lax
from jax.experimental import pallas as pl
from jax.experimental.pallas import tpu as pltpu
from jax.sharding import Mesh, PartitionSpec as P

X = ("x",)
Y = ("h", "l")
F32 = jnp.float32
BF16 = jnp.bfloat16
LOG2E = 1.4426950408889634
WHOLE = pl.BlockSpec(memory_space=pltpu.VMEM)
PARAMS = pltpu.CompilerParams(vmem_limit_bytes=12 * 2**20)


def call(body, out_shape, *operands):
    return pl.pallas_call(
        body,
        out_shape=out_shape,
        in_specs=[WHOLE] * len(operands),
        out_specs=jax.tree.map(lambda _: WHOLE, out_shape),
        compiler_params=PARAMS,
    )(*operands)


def shaped(shape, kind):
    return jax.ShapeDtypeStruct(shape, kind)


def pack_body(quads, landmarks, whitening, out, land, white, sems):
    fetches = [pltpu.make_async_copy(landmarks, land, sems.at[0]), pltpu.make_async_copy(whitening, white, sems.at[1])]
    for fetch in fetches:
        fetch.start()
    for fetch in fetches:
        fetch.wait()
    rows = land.shape[0]
    part = rows // quads
    white32 = white[...].astype(F32)
    beside = jnp.concatenate([white32[q * part : (q + 1) * part] for q in range(quads)], axis=1).astype(BF16)
    for i in range(out.shape[0]):
        out[i, :rows] = land[...]
        out[i, rows:] = beside


def pack(landmarks, whitening, copies):
    rows, width = landmarks.shape
    quads = width // whitening.shape[1]
    return pl.pallas_call(
        functools.partial(pack_body, quads),
        out_shape=shaped((copies, rows + rows // quads, width), BF16),
        in_specs=[pl.BlockSpec(memory_space=pltpu.HBM)] * 2,
        scratch_shapes=[
            pltpu.VMEM(landmarks.shape, BF16),
            pltpu.VMEM(whitening.shape, BF16),
            pltpu.SemaphoreType.DMA((2,)),
        ],
        compiler_params=PARAMS,
    )(*[pltpu.with_memory_space_constraint(array, pltpu.HBM) for array in (landmarks, whitening)])


def unpack(block, rank):
    count, packed, width = block.shape
    quads = width // rank
    rows = packed * quads // (quads + 1)
    land = block[:, :rows].reshape(count * rows, width)
    white = block[:, rows:].astype(F32)
    white = jnp.stack([white[:, :, q * rank : (q + 1) * rank] for q in range(quads)], axis=1)
    return land, white.reshape(count * rows, rank).astype(BF16)


def pieces_of(stacks, members):
    for stack in stacks:
        for i in range(0, stack.shape[0], members):
            yield stack[i : i + members]


def prepare_body(parts, places, features, cot_t, feat, feat_t, sq_feat, cot):
    own = features.shape[0] // parts
    for i, place in enumerate(places()):
        start = pl.multiple_of(place * own, own)
        to = slice(i * own, (i + 1) * own)
        some = features[pl.ds(start, own), :]
        turned = some.T
        turned32 = turned.astype(F32)
        feat[to, :] = some
        feat_t[:, to] = turned
        sq_feat[:, to] = jnp.sum(turned32 * turned32, axis=0, keepdims=True)
        cot[:, to] = cot_t[:, pl.ds(start, own)].astype(F32)


def prepare(features, cot_t, parts, places, count):
    toks, width = features.shape
    toks = toks // parts * count
    rank = cot_t.shape[0]
    shapes = [shaped((toks, width), BF16), shaped((width, toks), BF16), shaped((1, toks), F32), shaped((rank, toks), F32)]
    return call(functools.partial(prepare_body, parts, places), shapes, features, cot_t)


def forward_body(count, members, rank, first, *refs):
    stacks, (feat_t, sq_feat), outs = refs[:count], refs[count : count + 2], refs[count + 2 + (not first) :]
    blocks = sum(stack.shape[0] for stack in stacks) // members
    kerns, embeds = outs[:blocks], outs[blocks:]
    width = feat_t.shape[0]
    scale = 4.0 / width * LOG2E
    bias = sq_feat[...] * (-scale)
    total = None if first else refs[count + 2][...]
    for block, kern in zip(pieces_of(stacks, members), kerns):
        land, white = unpack(block, rank)
        land32 = land.astype(F32)
        sq_land = jnp.sum(land32 * land32, axis=1, keepdims=True) * (-scale)
        cross = jnp.dot(land, feat_t[...], preferred_element_type=F32)
        value = jnp.exp2(cross * (2.0 * scale) + (bias + sq_land)).astype(BF16)
        kern[...] = value
        part = lax.dot_general(white, value, (((0,), (0,)), ((), ())), preferred_element_type=F32)
        total = part if total is None else total + part
    for embed in embeds:
        embed[...] = total.astype(embed.dtype)


def forward(blocks, members, feat_t, sq_feat, prior, last, rank):
    width, toks = feat_t.shape
    count = sum(block.shape[0] for block in blocks) // members
    rows = sum(block.size for block in blocks) // (width + rank) // count
    shapes = [shaped((rows, toks), BF16)] * count + [shaped((rank, toks), kind) for kind in ([F32, BF16] if last else [F32])]
    outs = call(functools.partial(forward_body, len(blocks), members, rank, not prior), shapes, *blocks, feat_t, sq_feat, *prior)
    return outs[:count], outs[count:]


def moved(ref, place, places, bit):
    own = ref.shape[1] // places
    start = (place ^ bit) * own
    return ref[:, start : start + own].astype(F32)


def pair_sum_body(places, share, other, total, rounded):
    own = share.shape[1] // places
    for p in range(places):
        at = slice(p * own, (p + 1) * own)
        total[:, at] = share[:, at] + moved(other, p, places, 1)
    rounded[...] = total[...].astype(BF16)


def pair_sum(share, other, places):
    shapes = [shaped(share.shape, F32), shaped(share.shape, BF16)]
    return call(functools.partial(pair_sum_body, places), shapes, share, other)


def norm_body(factor, places, share, other, cot, out):
    own = cot.shape[1] // places
    for p in range(places):
        at = slice(p * own, (p + 1) * own)
        embed = share[:, at] + moved(other, p, places, 2)
        upstream = cot[:, at]
        scale = lax.rsqrt(jnp.mean(embed * embed, axis=0, keepdims=True) + 1e-06)
        normed = embed * scale
        grad = scale * (upstream - normed * jnp.mean(upstream * normed, axis=0, keepdims=True))
        out[:, at] = (factor * grad).astype(BF16)


def norm_backward(share, other, cot, factor, places):
    return call(functools.partial(norm_body, factor, places), shaped(cot.shape, BF16), share, other, cot)


def backward_body(count, members, rank, first, *refs):
    stacks, refs = refs[:count], refs[count:]
    blocks = sum(stack.shape[0] for stack in stacks) // members
    kerns, (dembed, feat) = refs[:blocks], refs[blocks : blocks + 2]
    coef, land_grad, row_total = refs[-3:]
    total = None if first else refs[blocks + 2][...]
    for i, block in enumerate(pieces_of(stacks, members)):
        land, white = unpack(block, rank)
        rows = land.shape[0]
        at = slice(i * rows, (i + 1) * rows)
        dkernel = jnp.dot(white, dembed[...], preferred_element_type=F32)
        value = (dkernel * kerns[i][...].astype(F32)).astype(BF16)
        coef[at, :] = value
        value32 = value.astype(F32)
        part = jnp.sum(value32, axis=0, keepdims=True)
        total = part if total is None else total + part
        col_total = jnp.sum(value32, axis=1, keepdims=True)
        pulled = jnp.dot(value, feat[...], preferred_element_type=F32)
        land_grad[at, :] = (2.0 * (col_total * land.astype(F32) - pulled)).astype(land_grad.dtype)
    row_total[...] = total


def backward(blocks, members, kerns, dembed, feat, prior, kind):
    toks, width = feat.shape
    rows = sum(kern.shape[0] for kern in kerns)
    shapes = [shaped((rows, toks), BF16), shaped((rows, width), kind), shaped((1, toks), F32)]
    body = functools.partial(backward_body, len(blocks), members, dembed.shape[0], not prior)
    return call(body, shapes, *blocks, *kerns, dembed, feat, *prior)


def feature_body(count, members, coefs, rank, *refs):
    stacks, coef, (feat_t, row_total), outs = refs[:count], refs[count : count + coefs], refs[count + coefs : count + coefs + 2], refs[count + coefs + 2 :]
    each = sum(stack.shape[0] for stack in stacks) // members // coefs
    pulled = None
    for i, block in enumerate(pieces_of(stacks, members)):
        land, _ = unpack(block, rank)
        rows = land.shape[0]
        at = slice(i % each * rows, (i % each + 1) * rows)
        part = lax.dot_general(land, coef[i // each][at, :], (((0,), (0,)), ((), ())), preferred_element_type=F32)
        pulled = part if pulled is None else pulled + part
    grad = 2.0 * (row_total[...] * feat_t[...].astype(F32) - pulled)
    start = 0
    for out in outs:
        out[...] = grad[:, start : start + out.shape[1]].astype(out.dtype)
        start += out.shape[1]


def feature_share(blocks, members, coefs, feat_t, row_total, parts, rank):
    width, toks = feat_t.shape
    shapes = [shaped((width, toks // parts), kind) for kind in [F32] + [BF16] * (parts - 1)]
    body = functools.partial(feature_body, len(blocks), members, len(coefs), rank)
    return call(body, shapes, *blocks, *coefs, feat_t, row_total)


def shift(block, axes, step):
    size = lax.axis_size(axes)
    return lax.ppermute(block, axes, [(i, (i + step) % size) for i in range(size)])


def partner(block, ring, which):
    masks = (1, 3)
    perm = [(2 * i + c, 2 * (i ^ masks[which ^ c]) + c) for i in range(lax.axis_size(ring)) for c in range(2)]
    return lax.ppermute(block, ring + ("c",), perm)


def spread(block, axes):
    return [block] + [shift(block, axes, s) for s in range(1, lax.axis_size(axes))]


def collect(pieces, axes, direction):
    total = pieces[0]
    for s in range(1, lax.axis_size(axes)):
        total = total + shift(pieces[s].astype(BF16), axes, direction * s).astype(F32)
    return total


def collect_at_once(pieces, axes):
    return jnp.sum(lax.all_to_all(pieces.astype(BF16), axes, 0, 0, tiled=True).astype(F32), axis=0)


def per_device(features, landmarks, whitening, cotangent):
    toks, width = features.shape
    rank = whitening.shape[1]
    n_x, n_h, n_y, n_z = lax.axis_size("x"), lax.axis_size("h"), lax.axis_size(Y), lax.axis_size("z")
    rows = landmarks.shape[0]
    gamma = 4.0 / width

    def places():
        here, half, core = lax.axis_index("x"), lax.axis_index("h"), lax.axis_index("c")
        members = [here, here ^ (1 + 2 * core), here ^ (3 - 2 * core), here ^ 2]
        return [member * n_h + half for member in members]

    packed = lax.all_to_all(pack(landmarks, whitening, n_z), "z", 0, 0, tiled=True)
    feat, feat_t, sq_feat, cot = prepare(features, cotangent.T, n_x * n_h, places, n_x)
    packed, feat, feat_t, sq_feat, cot = lax.optimization_barrier((packed, feat, feat_t, sq_feat, cot))
    mine = spread(packed, Y)

    kern_own, embed = forward(mine[:1], n_z, feat_t, sq_feat, [], False, rank)
    *arrived, embed = lax.optimization_barrier((*mine[1:], *embed))
    mine = mine[:1] + arrived
    theirs = [shift(jnp.concatenate(mine, axis=0), "c", 1)]
    kern_mine, embed = forward(arrived, n_z, feat_t, sq_feat, [embed], False, rank)
    kern_theirs, (embed, share) = forward(theirs, n_z, feat_t, sq_feat, embed, True, rank)
    kern_mine = kern_own + kern_mine
    embed, share = pair_sum(embed, partner(share, X, 0), n_x)
    dembed = norm_backward(embed, partner(share, X, 1), cot, -gamma, n_x)

    coef_theirs, land_theirs, row_total = backward(theirs, n_z, kern_theirs, dembed, feat, [], BF16)
    coef_mine, land_mine, row_total = backward(mine, n_z, kern_mine, dembed, feat, [row_total], F32)
    land_share = (land_mine + shift(land_theirs, "c", 1).astype(F32)).reshape(n_y, n_z, rows, width)
    land_share = collect(land_share, Y, -1)

    own, first, second, opposite = feature_share(mine + theirs, n_z, [coef_mine, coef_theirs], feat_t, row_total, n_x, rank)
    landmark_grad = collect_at_once(land_share, "z")
    arrived = [partner(first, X, 0), partner(second, X, 1), shift(opposite, "x", 2)]
    feature_grad = (own + sum(share.astype(F32) for share in arrived)).T
    return (feature_grad, landmark_grad)


def solution(mesh):
    fine = Mesh(mesh.devices.reshape(4, 2, 2, 8, 2), ("x", "h", "l", "z", "c"))
    lm, tx = ("x", "h"), ("l", "z", "c")
    placed = (P(tx, None), P(lm + tx, None), P(lm + tx, None), P(tx, None))
    return jax.shard_map(
        per_device,
        mesh=fine,
        in_specs=placed,
        out_specs=(P(tx + lm, None), P(lm + tx, None)),
        check_vma=False,
    )
```

```python
import functools

import jax
import jax.numpy as jnp
from jax import lax
from jax.experimental import pallas as pl
from jax.experimental.pallas import tpu as pltpu
from jax.sharding import Mesh, PartitionSpec as P

X = ("x",)
Y = ("h", "l")
F32 = jnp.float32
BF16 = jnp.bfloat16
LOG2E = 1.4426950408889634
WHOLE = pl.BlockSpec(memory_space=pltpu.VMEM)
PARAMS = pltpu.CompilerParams(vmem_limit_bytes=12 * 2**20)


def call(body, out_shape, *operands):
    return pl.pallas_call(
        body,
        out_shape=out_shape,
        in_specs=[WHOLE] * len(operands),
        out_specs=jax.tree.map(lambda _: WHOLE, out_shape),
        compiler_params=PARAMS,
    )(*operands)


def shaped(shape, kind):
    return jax.ShapeDtypeStruct(shape, kind)


def pack_body(quads, landmarks, whitening, out, land, white, sems):
    fetches = [pltpu.make_async_copy(landmarks, land, sems.at[0]), pltpu.make_async_copy(whitening, white, sems.at[1])]
    for fetch in fetches:
        fetch.start()
    for fetch in fetches:
        fetch.wait()
    rows = land.shape[0]
    part = rows // quads
    white32 = white[...].astype(F32)
    beside = jnp.concatenate([white32[q * part : (q + 1) * part] for q in range(quads)], axis=1).astype(BF16)
    for i in range(out.shape[0]):
        out[i, :rows] = land[...]
        out[i, rows:] = beside


def pack(landmarks, whitening, copies):
    rows, width = landmarks.shape
    quads = width // whitening.shape[1]
    return pl.pallas_call(
        functools.partial(pack_body, quads),
        out_shape=shaped((copies, rows + rows // quads, width), BF16),
        in_specs=[pl.BlockSpec(memory_space=pltpu.HBM)] * 2,
        scratch_shapes=[
            pltpu.VMEM(landmarks.shape, BF16),
            pltpu.VMEM(whitening.shape, BF16),
            pltpu.SemaphoreType.DMA((2,)),
        ],
        compiler_params=PARAMS,
    )(*[pltpu.with_memory_space_constraint(array, pltpu.HBM) for array in (landmarks, whitening)])


def unpack(block, rank):
    count, packed, width = block.shape
    quads = width // rank
    rows = packed * quads // (quads + 1)
    land = block[:, :rows].reshape(count * rows, width)
    white = block[:, rows:].astype(F32)
    white = jnp.stack([white[:, :, q * rank : (q + 1) * rank] for q in range(quads)], axis=1)
    return land, white.reshape(count * rows, rank).astype(BF16)


def pieces_of(stacks, members):
    for stack in stacks:
        for i in range(0, stack.shape[0], members):
            yield stack[i : i + members]


def prepare_body(parts, places, features, cot_t, feat, feat_t, sq_feat, cot):
    own = features.shape[0] // parts
    for i, place in enumerate(places()):
        start = pl.multiple_of(place * own, own)
        to = slice(i * own, (i + 1) * own)
        some = features[pl.ds(start, own), :]
        turned = some.T
        turned32 = turned.astype(F32)
        feat[to, :] = some
        feat_t[:, to] = turned
        sq_feat[:, to] = jnp.sum(turned32 * turned32, axis=0, keepdims=True)
        cot[:, to] = cot_t[:, pl.ds(start, own)].astype(F32)


def prepare(features, cot_t, parts, places, count):
    toks, width = features.shape
    toks = toks // parts * count
    rank = cot_t.shape[0]
    shapes = [shaped((toks, width), BF16), shaped((width, toks), BF16), shaped((1, toks), F32), shaped((rank, toks), F32)]
    return call(functools.partial(prepare_body, parts, places), shapes, features, cot_t)


def forward_body(count, members, rank, first, *refs):
    stacks, (feat_t, sq_feat), outs = refs[:count], refs[count : count + 2], refs[count + 2 + (not first) :]
    blocks = sum(stack.shape[0] for stack in stacks) // members
    kerns, embeds = outs[:blocks], outs[blocks:]
    width = feat_t.shape[0]
    scale = 4.0 / width * LOG2E
    bias = sq_feat[...] * (-scale)
    total = None if first else refs[count + 2][...]
    whites, values = [], []
    for block, kern in zip(pieces_of(stacks, members), kerns):
        land, white = unpack(block, rank)
        land32 = land.astype(F32)
        sq_land = jnp.sum(land32 * land32, axis=1, keepdims=True) * (-scale)
        cross = jnp.dot(land, feat_t[...], preferred_element_type=F32)
        value = jnp.exp2(cross * (2.0 * scale) + (bias + sq_land))
        kern[...] = value
        values.append(value.astype(BF16))
        whites.append(white.T)
    for white, value in zip(whites, values):
        part = jnp.dot(white, value, preferred_element_type=F32)
        total = part if total is None else total + part
    for embed in embeds:
        embed[...] = total.astype(embed.dtype)


def forward(blocks, members, feat_t, sq_feat, prior, last, rank):
    width, toks = feat_t.shape
    count = sum(block.shape[0] for block in blocks) // members
    rows = sum(block.size for block in blocks) // (width + rank) // count
    shapes = [shaped((rows, toks), F32)] * count + [shaped((rank, toks), kind) for kind in ([F32, BF16] if last else [F32])]
    outs = call(functools.partial(forward_body, len(blocks), members, rank, not prior), shapes, *blocks, feat_t, sq_feat, *prior)
    return outs[:count], outs[count:]


def moved(ref, place, places, bit):
    own = ref.shape[1] // places
    start = (place ^ bit) * own
    return ref[:, start : start + own].astype(F32)


def pair_sum_body(places, share, other, total, rounded):
    own = share.shape[1] // places
    for p in range(places):
        at = slice(p * own, (p + 1) * own)
        total[:, at] = share[:, at] + moved(other, p, places, 1)
    rounded[...] = total[...].astype(BF16)


def pair_sum(share, other, places):
    shapes = [shaped(share.shape, F32), shaped(share.shape, BF16)]
    return call(functools.partial(pair_sum_body, places), shapes, share, other)


def norm_body(factor, places, share, other, cot, out):
    own = cot.shape[1] // places
    for p in range(places):
        at = slice(p * own, (p + 1) * own)
        embed = share[:, at] + moved(other, p, places, 2)
        upstream = cot[:, at]
        scale = lax.rsqrt(jnp.mean(embed * embed, axis=0, keepdims=True) + 1e-06)
        normed = embed * scale
        grad = scale * (upstream - normed * jnp.mean(upstream * normed, axis=0, keepdims=True))
        out[:, at] = (factor * grad).astype(BF16)


def norm_backward(share, other, cot, factor, places):
    return call(functools.partial(norm_body, factor, places), shaped(cot.shape, BF16), share, other, cot)


def backward_body(count, members, rank, first, *refs):
    stacks, refs = refs[:count], refs[count:]
    blocks = sum(stack.shape[0] for stack in stacks) // members
    kerns, (dembed, feat) = refs[:blocks], refs[blocks : blocks + 2]
    coef, land_grad, row_total = refs[-3:]
    total = None if first else refs[blocks + 2][...]
    for i, block in enumerate(pieces_of(stacks, members)):
        land, white = unpack(block, rank)
        rows = land.shape[0]
        at = slice(i * rows, (i + 1) * rows)
        dkernel = jnp.dot(white, dembed[...], preferred_element_type=F32)
        value32 = dkernel * kerns[i][...]
        value = value32.astype(BF16)
        coef[at, :] = value
        part = jnp.sum(value32, axis=0, keepdims=True)
        total = part if total is None else total + part
        col_total = jnp.sum(value32, axis=1, keepdims=True)
        pulled = jnp.dot(value, feat[...], preferred_element_type=F32)
        land_grad[at, :] = (2.0 * (col_total * land.astype(F32) - pulled)).astype(land_grad.dtype)
    row_total[...] = total


def backward(blocks, members, kerns, dembed, feat, prior, kind):
    toks, width = feat.shape
    rows = sum(kern.shape[0] for kern in kerns)
    shapes = [shaped((rows, toks), BF16), shaped((rows, width), kind), shaped((1, toks), F32)]
    body = functools.partial(backward_body, len(blocks), members, dembed.shape[0], not prior)
    return call(body, shapes, *blocks, *kerns, dembed, feat, *prior)


def feature_body(count, members, coefs, rank, *refs):
    stacks, coef, (feat_t, row_total), outs = refs[:count], refs[count : count + coefs], refs[count + coefs : count + coefs + 2], refs[count + coefs + 2 :]
    each = sum(stack.shape[0] for stack in stacks) // members // coefs
    pulled = None
    for i, block in enumerate(pieces_of(stacks, members)):
        land, _ = unpack(block, rank)
        rows = land.shape[0]
        at = slice(i % each * rows, (i % each + 1) * rows)
        part = lax.dot_general(land, coef[i // each][at, :], (((0,), (0,)), ((), ())), preferred_element_type=F32)
        pulled = part if pulled is None else pulled + part
    grad = 2.0 * (row_total[...] * feat_t[...].astype(F32) - pulled)
    start = 0
    for out in outs:
        out[...] = grad[:, start : start + out.shape[1]].astype(out.dtype)
        start += out.shape[1]


def feature_share(blocks, members, coefs, feat_t, row_total, parts, rank):
    width, toks = feat_t.shape
    shapes = [shaped((width, toks // parts), kind) for kind in [F32] + [BF16] * (parts - 1)]
    body = functools.partial(feature_body, len(blocks), members, len(coefs), rank)
    return call(body, shapes, *blocks, *coefs, feat_t, row_total)


def shift(block, axes, step):
    size = lax.axis_size(axes)
    return lax.ppermute(block, axes, [(i, (i + step) % size) for i in range(size)])


def partner(block, ring, which):
    masks = (1, 3)
    perm = [(2 * i + c, 2 * (i ^ masks[which ^ c]) + c) for i in range(lax.axis_size(ring)) for c in range(2)]
    return lax.ppermute(block, ring + ("c",), perm)


def spread(block, axes):
    return [block] + [shift(block, axes, s) for s in range(1, lax.axis_size(axes))]


def collect(pieces, axes, direction):
    total = pieces[0]
    for s in range(1, lax.axis_size(axes)):
        total = total + shift(pieces[s].astype(BF16), axes, direction * s).astype(F32)
    return total


def collect_at_once(pieces, axes):
    return jnp.sum(lax.all_to_all(pieces.astype(BF16), axes, 0, 0, tiled=True).astype(F32), axis=0)


def per_device(features, landmarks, whitening, cotangent):
    toks, width = features.shape
    rank = whitening.shape[1]
    n_x, n_h, n_y, n_z = lax.axis_size("x"), lax.axis_size("h"), lax.axis_size(Y), lax.axis_size("z")
    rows = landmarks.shape[0]
    gamma = 4.0 / width

    def places():
        here, half, core = lax.axis_index("x"), lax.axis_index("h"), lax.axis_index("c")
        members = [here, here ^ (1 + 2 * core), here ^ (3 - 2 * core), here ^ 2]
        return [member * n_h + half for member in members]

    packed = lax.all_to_all(pack(landmarks, whitening, n_z), "z", 0, 0, tiled=True)
    feat, feat_t, sq_feat, cot = prepare(features, cotangent.T, n_x * n_h, places, n_x)
    packed, feat, feat_t, sq_feat, cot = lax.optimization_barrier((packed, feat, feat_t, sq_feat, cot))
    mine = spread(packed, Y)

    kern_own, embed = forward(mine[:1], n_z, feat_t, sq_feat, [], False, rank)
    *arrived, embed = lax.optimization_barrier((*mine[1:], *embed))
    mine = mine[:1] + arrived
    theirs = [shift(jnp.concatenate(mine, axis=0), "c", 1)]
    kern_mine, embed = forward(arrived, n_z, feat_t, sq_feat, [embed], False, rank)
    kern_theirs, (embed, share) = forward(theirs, n_z, feat_t, sq_feat, embed, True, rank)
    kern_mine = kern_own + kern_mine
    embed, share = pair_sum(embed, partner(share, X, 0), n_x)
    dembed = norm_backward(embed, partner(share, X, 1), cot, -gamma, n_x)

    coef_theirs, land_theirs, row_total = backward(theirs, n_z, kern_theirs, dembed, feat, [], BF16)
    coef_mine, land_mine, row_total = backward(mine, n_z, kern_mine, dembed, feat, [row_total], F32)
    land_share = (land_mine + shift(land_theirs, "c", 1).astype(F32)).reshape(n_y, n_z, rows, width)
    land_share = collect(land_share, Y, -1)

    own, first, second, opposite = feature_share(mine + theirs, n_z, [coef_mine, coef_theirs], feat_t, row_total, n_x, rank)
    landmark_grad = collect_at_once(land_share, "z")
    arrived = [partner(first, X, 0), partner(second, X, 1), shift(opposite, "x", 2)]
    feature_grad = (own + sum(share.astype(F32) for share in arrived)).T
    return (feature_grad, landmark_grad)


def solution(mesh):
    fine = Mesh(mesh.devices.reshape(4, 2, 2, 8, 2), ("x", "h", "l", "z", "c"))
    lm, tx = ("x", "h"), ("l", "z", "c")
    placed = (P(tx, None), P(lm + tx, None), P(lm + tx, None), P(tx, None))
    return jax.shard_map(
        per_device,
        mesh=fine,
        in_specs=placed,
        out_specs=(P(tx + lm, None), P(lm + tx, None)),
        check_vma=False,
    )
```

```python
import functools

import jax
import jax.numpy as jnp
from jax import lax
from jax.experimental import pallas as pl
from jax.experimental.pallas import tpu as pltpu
from jax.sharding import Mesh, PartitionSpec as P

X = ("x",)
Y = ("h", "l")
F32 = jnp.float32
BF16 = jnp.bfloat16
LOG2E = 1.4426950408889634
WHOLE = pl.BlockSpec(memory_space=pltpu.VMEM)
PARAMS = pltpu.CompilerParams(vmem_limit_bytes=12 * 2**20)


def call(body, out_shape, *operands):
    return pl.pallas_call(
        body,
        out_shape=out_shape,
        in_specs=[WHOLE] * len(operands),
        out_specs=jax.tree.map(lambda _: WHOLE, out_shape),
        compiler_params=PARAMS,
    )(*operands)


def shaped(shape, kind):
    return jax.ShapeDtypeStruct(shape, kind)


def pack_body(quads, landmarks, whitening, out, land, white, sems):
    fetches = [pltpu.make_async_copy(landmarks, land, sems.at[0]), pltpu.make_async_copy(whitening, white, sems.at[1])]
    for fetch in fetches:
        fetch.start()
    for fetch in fetches:
        fetch.wait()
    rows = land.shape[0]
    part = rows // quads
    white32 = white[...].astype(F32)
    beside = jnp.concatenate([white32[q * part : (q + 1) * part] for q in range(quads)], axis=1).astype(BF16)
    for i in range(out.shape[0]):
        out[i, :rows] = land[...]
        out[i, rows:] = beside


def pack(landmarks, whitening, copies):
    rows, width = landmarks.shape
    quads = width // whitening.shape[1]
    return pl.pallas_call(
        functools.partial(pack_body, quads),
        out_shape=shaped((copies, rows + rows // quads, width), BF16),
        in_specs=[pl.BlockSpec(memory_space=pltpu.HBM)] * 2,
        scratch_shapes=[
            pltpu.VMEM(landmarks.shape, BF16),
            pltpu.VMEM(whitening.shape, BF16),
            pltpu.SemaphoreType.DMA((2,)),
        ],
        compiler_params=PARAMS,
    )(*[pltpu.with_memory_space_constraint(array, pltpu.HBM) for array in (landmarks, whitening)])


def unpack(block, rank):
    count, packed, width = block.shape
    quads = width // rank
    rows = packed * quads // (quads + 1)
    land = block[:, :rows].reshape(count * rows, width)
    white = block[:, rows:].astype(F32)
    white = jnp.stack([white[:, :, q * rank : (q + 1) * rank] for q in range(quads)], axis=1)
    return land, white.reshape(count * rows, rank).astype(BF16)


def pieces_of(stacks, members):
    for stack in stacks:
        for i in range(0, stack.shape[0], members):
            yield stack[i : i + members]


def prepare_body(parts, places, features, cot_t, feat, feat_t, sq_feat, cot):
    own = features.shape[0] // parts
    for i, place in enumerate(places()):
        start = pl.multiple_of(place * own, own)
        to = slice(i * own, (i + 1) * own)
        some = features[pl.ds(start, own), :]
        turned = some.T
        turned32 = turned.astype(F32)
        feat[to, :] = some
        feat_t[:, to] = turned
        sq_feat[:, to] = jnp.sum(turned32 * turned32, axis=0, keepdims=True)
        cot[:, to] = cot_t[:, pl.ds(start, own)].astype(F32)


def prepare(features, cot_t, parts, places, count):
    toks, width = features.shape
    toks = toks // parts * count
    rank = cot_t.shape[0]
    shapes = [shaped((toks, width), BF16), shaped((width, toks), BF16), shaped((1, toks), F32), shaped((rank, toks), F32)]
    return call(functools.partial(prepare_body, parts, places), shapes, features, cot_t)


def forward_body(count, members, rank, first, *refs):
    stacks, (feat_t, sq_feat), outs = refs[:count], refs[count : count + 2], refs[count + 2 + (not first) :]
    blocks = sum(stack.shape[0] for stack in stacks) // members
    kerns, embeds = outs[:blocks], outs[blocks:]
    width = feat_t.shape[0]
    scale = 4.0 / width * LOG2E
    bias = sq_feat[...] * (-scale)
    total = None if first else refs[count + 2][...]
    whites, values = [], []
    for block, kern in zip(pieces_of(stacks, members), kerns):
        land, white = unpack(block, rank)
        land32 = land.astype(F32)
        sq_land = jnp.sum(land32 * land32, axis=1, keepdims=True) * (-scale)
        cross = jnp.dot(land, feat_t[...], preferred_element_type=F32)
        value = jnp.exp2(cross * (2.0 * scale) + (bias + sq_land))
        kern[...] = value
        values.append(value.astype(BF16))
        whites.append(white.T)
    for white, value in zip(whites, values):
        part = jnp.dot(white, value, preferred_element_type=F32)
        total = part if total is None else total + part
    for embed in embeds:
        embed[...] = total.astype(embed.dtype)


def forward(blocks, members, feat_t, sq_feat, prior, last, rank):
    width, toks = feat_t.shape
    count = sum(block.shape[0] for block in blocks) // members
    rows = sum(block.size for block in blocks) // (width + rank) // count
    shapes = [shaped((rows, toks), F32)] * count + [shaped((rank, toks), kind) for kind in ([F32, BF16] if last else [F32])]
    outs = call(functools.partial(forward_body, len(blocks), members, rank, not prior), shapes, *blocks, feat_t, sq_feat, *prior)
    return outs[:count], outs[count:]


def moved(ref, place, places, bit):
    own = ref.shape[1] // places
    start = (place ^ bit) * own
    return ref[:, start : start + own].astype(F32)


def pair_sum_body(places, share, other, total, rounded):
    own = share.shape[1] // places
    for p in range(places):
        at = slice(p * own, (p + 1) * own)
        total[:, at] = share[:, at] + moved(other, p, places, 1)
    rounded[...] = total[...].astype(BF16)


def pair_sum(share, other, places):
    shapes = [shaped(share.shape, F32), shaped(share.shape, BF16)]
    return call(functools.partial(pair_sum_body, places), shapes, share, other)


def norm_backward(factor, places, share, other, cot, out):
    own = cot.shape[1] // places
    for p in range(places):
        at = slice(p * own, (p + 1) * own)
        embed = share[:, at] + moved(other, p, places, 2)
        upstream = cot[:, at]
        scale = lax.rsqrt(jnp.mean(embed * embed, axis=0, keepdims=True) + 1e-06)
        normed = embed * scale
        grad = scale * (upstream - normed * jnp.mean(upstream * normed, axis=0, keepdims=True))
        out[:, at] = (factor * grad).astype(BF16)


def backward_body(count, members, rank, first, *refs):
    stacks, refs = refs[:count], refs[count:]
    blocks = sum(stack.shape[0] for stack in stacks) // members
    kerns, (dembed, feat) = refs[:blocks], refs[blocks : blocks + 2]
    coef, land_grad, row_total = refs[-3:]
    total = None if first else refs[blocks + 2][...]
    for i, block in enumerate(pieces_of(stacks, members)):
        land, white = unpack(block, rank)
        rows = land.shape[0]
        at = slice(i * rows, (i + 1) * rows)
        dkernel = jnp.dot(white, dembed[...], preferred_element_type=F32)
        value32 = dkernel * kerns[i][...]
        value = value32.astype(BF16)
        coef[at, :] = value
        part = jnp.sum(value32, axis=0, keepdims=True)
        total = part if total is None else total + part
        col_total = jnp.sum(value32, axis=1, keepdims=True)
        pulled = jnp.dot(value, feat[...], preferred_element_type=F32)
        land_grad[at, :] = (2.0 * (col_total * land.astype(F32) - pulled)).astype(land_grad.dtype)
    row_total[...] = total


def backward_first_body(count, members, rank, factor, places, *refs):
    *ins, share, other, cot, feat, coef, land_grad, row_total, dembed = refs
    norm_backward(factor, places, share, other, cot, dembed)
    backward_body(count, members, rank, True, *ins, dembed, feat, coef, land_grad, row_total)


def backward_shapes(kerns, feat, kind):
    toks, width = feat.shape
    rows = sum(kern.shape[0] for kern in kerns)
    return [shaped((rows, toks), BF16), shaped((rows, width), kind), shaped((1, toks), F32)]


def backward_first(blocks, members, kerns, shares, cot, feat, factor, places):
    rank = cot.shape[0]
    body = functools.partial(backward_first_body, len(blocks), members, rank, factor, places)
    shapes = backward_shapes(kerns, feat, BF16) + [shaped(cot.shape, BF16)]
    return call(body, shapes, *blocks, *kerns, *shares, cot, feat)


def backward(blocks, members, kerns, dembed, feat, prior):
    body = functools.partial(backward_body, len(blocks), members, dembed.shape[0], False)
    return call(body, backward_shapes(kerns, feat, F32), *blocks, *kerns, dembed, feat, prior)


def feature_body(count, members, coefs, rank, *refs):
    stacks, coef, (feat_t, row_total), outs = refs[:count], refs[count : count + coefs], refs[count + coefs : count + coefs + 2], refs[count + coefs + 2 :]
    each = sum(stack.shape[0] for stack in stacks) // members // coefs
    pulled = None
    for i, block in enumerate(pieces_of(stacks, members)):
        land, _ = unpack(block, rank)
        rows = land.shape[0]
        at = slice(i % each * rows, (i % each + 1) * rows)
        part = lax.dot_general(land, coef[i // each][at, :], (((0,), (0,)), ((), ())), preferred_element_type=F32)
        pulled = part if pulled is None else pulled + part
    grad = 2.0 * (row_total[...] * feat_t[...].astype(F32) - pulled)
    start = 0
    for out in outs:
        out[...] = grad[:, start : start + out.shape[1]].astype(out.dtype)
        start += out.shape[1]


def feature_share(blocks, members, coefs, feat_t, row_total, parts, rank):
    width, toks = feat_t.shape
    shapes = [shaped((width, toks // parts), kind) for kind in [F32] + [BF16] * (parts - 1)]
    body = functools.partial(feature_body, len(blocks), members, len(coefs), rank)
    return call(body, shapes, *blocks, *coefs, feat_t, row_total)


def shift(block, axes, step):
    size = lax.axis_size(axes)
    return lax.ppermute(block, axes, [(i, (i + step) % size) for i in range(size)])


def partner(block, ring, which):
    masks = (1, 3)
    perm = [(2 * i + c, 2 * (i ^ masks[which ^ c]) + c) for i in range(lax.axis_size(ring)) for c in range(2)]
    return lax.ppermute(block, ring + ("c",), perm)


def spread(block, axes):
    return [block] + [shift(block, axes, s) for s in range(1, lax.axis_size(axes))]


def collect(pieces, axes, direction):
    total = pieces[0]
    for s in range(1, lax.axis_size(axes)):
        total = total + shift(pieces[s].astype(BF16), axes, direction * s).astype(F32)
    return total


def collect_at_once(pieces, axes):
    return jnp.sum(lax.all_to_all(pieces.astype(BF16), axes, 0, 0, tiled=True).astype(F32), axis=0)


def per_device(features, landmarks, whitening, cotangent):
    toks, width = features.shape
    rank = whitening.shape[1]
    n_x, n_h, n_y, n_z = lax.axis_size("x"), lax.axis_size("h"), lax.axis_size(Y), lax.axis_size("z")
    rows = landmarks.shape[0]
    gamma = 4.0 / width

    def places():
        here, half, core = lax.axis_index("x"), lax.axis_index("h"), lax.axis_index("c")
        members = [here, here ^ (1 + 2 * core), here ^ (3 - 2 * core), here ^ 2]
        return [member * n_h + half for member in members]

    packed = lax.all_to_all(pack(landmarks, whitening, n_z), "z", 0, 0, tiled=True)
    feat, feat_t, sq_feat, cot = prepare(features, cotangent.T, n_x * n_h, places, n_x)
    packed, feat, feat_t, sq_feat, cot = lax.optimization_barrier((packed, feat, feat_t, sq_feat, cot))
    mine = spread(packed, Y)

    kern_own, embed = forward(mine[:1], n_z, feat_t, sq_feat, [], False, rank)
    *arrived, embed = lax.optimization_barrier((*mine[1:], *embed))
    mine = mine[:1] + arrived
    theirs = [shift(jnp.concatenate(mine, axis=0), "c", 1)]
    kern_mine, embed = forward(arrived, n_z, feat_t, sq_feat, [embed], False, rank)
    kern_theirs, (embed, share) = forward(theirs, n_z, feat_t, sq_feat, embed, True, rank)
    kern_mine = kern_own + kern_mine
    embed, share = pair_sum(embed, partner(share, X, 0), n_x)
    shares = [embed, partner(share, X, 1)]
    coef_theirs, land_theirs, row_total, dembed = backward_first(theirs, n_z, kern_theirs, shares, cot, feat, -gamma, n_x)
    coef_mine, land_mine, row_total = backward(mine, n_z, kern_mine, dembed, feat, row_total)
    land_share = (land_mine + shift(land_theirs, "c", 1).astype(F32)).reshape(n_y, n_z, rows, width)
    land_share = collect(land_share, Y, -1)

    own, first, second, opposite = feature_share(mine + theirs, n_z, [coef_mine, coef_theirs], feat_t, row_total, n_x, rank)
    landmark_grad = collect_at_once(land_share, "z")
    arrived = [partner(first, X, 0), partner(second, X, 1), shift(opposite, "x", 2)]
    feature_grad = (own + sum(share.astype(F32) for share in arrived)).T
    return (feature_grad, landmark_grad)


def solution(mesh):
    fine = Mesh(mesh.devices.reshape(4, 2, 2, 8, 2), ("x", "h", "l", "z", "c"))
    lm, tx = ("x", "h"), ("l", "z", "c")
    placed = (P(tx, None), P(lm + tx, None), P(lm + tx, None), P(tx, None))
    return jax.shard_map(
        per_device,
        mesh=fine,
        in_specs=placed,
        out_specs=(P(tx + lm, None), P(lm + tx, None)),
        check_vma=False,
    )
```

```python
import functools

import jax
import jax.numpy as jnp
from jax import lax
from jax.experimental import pallas as pl
from jax.experimental.pallas import tpu as pltpu
from jax.sharding import Mesh, PartitionSpec as P

X = ("x",)
Y = ("h", "l")
SHIFTS = (3, 1, 2)
F32 = jnp.float32
BF16 = jnp.bfloat16
LOG2E = 1.4426950408889634
WHOLE = pl.BlockSpec(memory_space=pltpu.VMEM)
PARAMS = pltpu.CompilerParams(vmem_limit_bytes=12 * 2**20)


def call(body, out_shape, *operands):
    return pl.pallas_call(
        body,
        out_shape=out_shape,
        in_specs=[WHOLE] * len(operands),
        out_specs=jax.tree.map(lambda _: WHOLE, out_shape),
        compiler_params=PARAMS,
    )(*operands)


def shaped(shape, kind):
    return jax.ShapeDtypeStruct(shape, kind)


def pack_body(quads, landmarks, whitening, out, land, white, sems):
    fetches = [pltpu.make_async_copy(landmarks, land, sems.at[0]), pltpu.make_async_copy(whitening, white, sems.at[1])]
    for fetch in fetches:
        fetch.start()
    for fetch in fetches:
        fetch.wait()
    rows = land.shape[0]
    part = rows // quads
    white32 = white[...].astype(F32)
    beside = jnp.concatenate([white32[q * part : (q + 1) * part] for q in range(quads)], axis=1).astype(BF16)
    for i in range(out.shape[0]):
        out[i, :rows] = land[...]
        out[i, rows:] = beside


def pack(landmarks, whitening, copies):
    rows, width = landmarks.shape
    quads = width // whitening.shape[1]
    return pl.pallas_call(
        functools.partial(pack_body, quads),
        out_shape=shaped((copies, rows + rows // quads, width), BF16),
        in_specs=[pl.BlockSpec(memory_space=pltpu.HBM)] * 2,
        scratch_shapes=[
            pltpu.VMEM(landmarks.shape, BF16),
            pltpu.VMEM(whitening.shape, BF16),
            pltpu.SemaphoreType.DMA((2,)),
        ],
        compiler_params=PARAMS,
    )(*[pltpu.with_memory_space_constraint(array, pltpu.HBM) for array in (landmarks, whitening)])


def unpack(block, rank):
    count, packed, width = block.shape
    quads = width // rank
    rows = packed * quads // (quads + 1)
    land = block[:, :rows].reshape(count * rows, width)
    white = block[:, rows:].astype(F32)
    white = jnp.stack([white[:, :, q * rank : (q + 1) * rank] for q in range(quads)], axis=1)
    return land, white.reshape(count * rows, rank).astype(BF16)


def pieces_of(stacks, members):
    for stack in stacks:
        for i in range(0, stack.shape[0], members):
            yield stack[i : i + members]


def prepare_body(parts, places, features, cot_t, feat, feat_t, sq_feat, cot):
    own = features.shape[0] // parts
    for i, place in enumerate(places()):
        start = pl.multiple_of(place * own, own)
        to = slice(i * own, (i + 1) * own)
        some = features[pl.ds(start, own), :]
        turned = some.T
        turned32 = turned.astype(F32)
        feat[to, :] = some
        feat_t[:, to] = turned
        sq_feat[:, to] = jnp.sum(turned32 * turned32, axis=0, keepdims=True)
        cot[:, to] = cot_t[:, pl.ds(start, own)].astype(F32)


def prepare(features, cot_t, parts, places, count):
    toks, width = features.shape
    toks = toks // parts * count
    rank = cot_t.shape[0]
    shapes = [shaped((toks, width), BF16), shaped((width, toks), BF16), shaped((1, toks), F32), shaped((rank, toks), F32)]
    return call(functools.partial(prepare_body, parts, places), shapes, features, cot_t)


def forward_body(count, members, rank, first, *refs):
    stacks, (feat_t, sq_feat), outs = refs[:count], refs[count : count + 2], refs[count + 2 + (not first) :]
    blocks = sum(stack.shape[0] for stack in stacks) // members
    kerns, embeds = outs[:blocks], outs[blocks:]
    width = feat_t.shape[0]
    scale = 4.0 / width * LOG2E
    bias = sq_feat[...] * (-scale)
    total = None if first else refs[count + 2][...]
    whites, values = [], []
    for block, kern in zip(pieces_of(stacks, members), kerns):
        land, white = unpack(block, rank)
        land32 = land.astype(F32)
        sq_land = jnp.sum(land32 * land32, axis=1, keepdims=True) * (-scale)
        cross = jnp.dot(land, feat_t[...], preferred_element_type=F32)
        value = jnp.exp2(cross * (2.0 * scale) + (bias + sq_land))
        kern[...] = value
        values.append(value.astype(BF16))
        whites.append(white.T)
    for white, value in zip(whites, values):
        part = jnp.dot(white, value, preferred_element_type=F32)
        total = part if total is None else total + part
    for embed in embeds:
        embed[...] = total.astype(embed.dtype)


def forward(blocks, members, feat_t, sq_feat, prior, last, rank):
    width, toks = feat_t.shape
    count = sum(block.shape[0] for block in blocks) // members
    rows = sum(block.size for block in blocks) // (width + rank) // count
    shapes = [shaped((rows, toks), F32)] * count + [shaped((rank, toks), kind) for kind in ([F32, BF16] if last else [F32])]
    outs = call(functools.partial(forward_body, len(blocks), members, rank, not prior), shapes, *blocks, feat_t, sq_feat, *prior)
    return outs[:count], outs[count:]


def moved(ref, place, places, bit):
    own = ref.shape[1] // places
    start = (place ^ bit) * own
    return ref[:, start : start + own].astype(F32)


def pair_sum_body(places, share, other, total, rounded):
    own = share.shape[1] // places
    for p in range(places):
        at = slice(p * own, (p + 1) * own)
        total[:, at] = share[:, at] + moved(other, p, places, 1)
    rounded[...] = total[...].astype(BF16)


def pair_sum(share, other, places):
    shapes = [shaped(share.shape, F32), shaped(share.shape, BF16)]
    return call(functools.partial(pair_sum_body, places), shapes, share, other)


def norm_body(factor, places, share, other, cot, out):
    own = cot.shape[1] // places
    for p in range(places):
        at = slice(p * own, (p + 1) * own)
        embed = share[:, at] + moved(other, p, places, 2)
        upstream = cot[:, at]
        scale = lax.rsqrt(jnp.mean(embed * embed, axis=0, keepdims=True) + 1e-06)
        normed = embed * scale
        grad = scale * (upstream - normed * jnp.mean(upstream * normed, axis=0, keepdims=True))
        out[:, at] = (factor * grad).astype(BF16)


def norm_backward(share, other, cot, factor, places):
    return call(functools.partial(norm_body, factor, places), shaped(cot.shape, BF16), share, other, cot)


def backward_body(count, members, rank, first, *refs):
    stacks, refs = refs[:count], refs[count:]
    blocks = sum(stack.shape[0] for stack in stacks) // members
    kerns, (dembed, feat) = refs[:blocks], refs[blocks : blocks + 2]
    coef, land_grad, row_total = refs[-3:]
    total = None if first else refs[blocks + 2][...]
    for i, block in enumerate(pieces_of(stacks, members)):
        land, white = unpack(block, rank)
        rows = land.shape[0]
        at = slice(i * rows, (i + 1) * rows)
        dkernel = jnp.dot(white, dembed[...], preferred_element_type=F32)
        value32 = dkernel * kerns[i][...]
        value = value32.astype(BF16)
        coef[at, :] = value
        part = jnp.sum(value32, axis=0, keepdims=True)
        total = part if total is None else total + part
        col_total = jnp.sum(value32, axis=1, keepdims=True)
        pulled = jnp.dot(value, feat[...], preferred_element_type=F32)
        land_grad[at, :] = (2.0 * (col_total * land.astype(F32) - pulled)).astype(land_grad.dtype)
    row_total[...] = total


def backward(blocks, members, kerns, dembed, feat, prior, kind):
    toks, width = feat.shape
    rows = sum(kern.shape[0] for kern in kerns)
    shapes = [shaped((rows, toks), BF16), shaped((rows, width), kind), shaped((1, toks), F32)]
    body = functools.partial(backward_body, len(blocks), members, dembed.shape[0], not prior)
    return call(body, shapes, *blocks, *kerns, dembed, feat, *prior)


def feature_body(count, members, coefs, rank, *refs):
    stacks, coef, (feat_t, row_total), outs = refs[:count], refs[count : count + coefs], refs[count + coefs : count + coefs + 2], refs[count + coefs + 2 :]
    each = sum(stack.shape[0] for stack in stacks) // members // coefs
    pulled = None
    for i, block in enumerate(pieces_of(stacks, members)):
        land, _ = unpack(block, rank)
        rows = land.shape[0]
        at = slice(i % each * rows, (i % each + 1) * rows)
        part = lax.dot_general(land, coef[i // each][at, :], (((0,), (0,)), ((), ())), preferred_element_type=F32)
        pulled = part if pulled is None else pulled + part
    grad = 2.0 * (row_total[...] * feat_t[...].astype(F32) - pulled)
    start = 0
    for out in outs:
        out[...] = grad[:, start : start + out.shape[1]].astype(out.dtype)
        start += out.shape[1]


def feature_share(blocks, members, coefs, feat_t, row_total, parts, rank):
    width, toks = feat_t.shape
    shapes = [shaped((width, toks // parts), kind) for kind in [F32] + [BF16] * (parts - 1)]
    body = functools.partial(feature_body, len(blocks), members, len(coefs), rank)
    return call(body, shapes, *blocks, *coefs, feat_t, row_total)


def shift(block, axes, step):
    size = lax.axis_size(axes)
    return lax.ppermute(block, axes, [(i, (i + step) % size) for i in range(size)])


def partner(block, ring, which):
    masks = (1, 3)
    perm = [(2 * i + c, 2 * (i ^ masks[which ^ c]) + c) for i in range(lax.axis_size(ring)) for c in range(2)]
    return lax.ppermute(block, ring + ("c",), perm)


def spread(block, axes):
    return [block] + [shift(block, axes, s) for s in SHIFTS]


def collect(pieces, axes):
    total = pieces[0]
    for i, s in enumerate(SHIFTS):
        total = total + shift(pieces[i + 1].astype(BF16), axes, -s).astype(F32)
    return total


def collect_at_once(pieces, axes):
    return jnp.sum(lax.all_to_all(pieces.astype(BF16), axes, 0, 0, tiled=True).astype(F32), axis=0)


def per_device(features, landmarks, whitening, cotangent):
    toks, width = features.shape
    rank = whitening.shape[1]
    n_x, n_h, n_y, n_z = lax.axis_size("x"), lax.axis_size("h"), lax.axis_size(Y), lax.axis_size("z")
    rows = landmarks.shape[0]
    gamma = 4.0 / width

    def places():
        here, half, core = lax.axis_index("x"), lax.axis_index("h"), lax.axis_index("c")
        members = [here, here ^ (1 + 2 * core), here ^ (3 - 2 * core), here ^ 2]
        return [member * n_h + half for member in members]

    packed = lax.all_to_all(pack(landmarks, whitening, n_z), "z", 0, 0, tiled=True)
    feat, feat_t, sq_feat, cot = prepare(features, cotangent.T, n_x * n_h, places, n_x)
    packed, feat, feat_t, sq_feat, cot = lax.optimization_barrier((packed, feat, feat_t, sq_feat, cot))
    mine = spread(packed, Y)

    kern_own, embed = forward(mine[:1], n_z, feat_t, sq_feat, [], False, rank)
    *arrived, embed = lax.optimization_barrier((*mine[1:], *embed))
    mine = mine[:1] + arrived
    theirs = [shift(jnp.concatenate(mine, axis=0), "c", 1)]
    kern_mine, embed = forward(arrived, n_z, feat_t, sq_feat, [embed], False, rank)
    kern_theirs, (embed, share) = forward(theirs, n_z, feat_t, sq_feat, embed, True, rank)
    kern_mine = kern_own + kern_mine
    embed, share = pair_sum(embed, partner(share, X, 0), n_x)
    dembed = norm_backward(embed, partner(share, X, 1), cot, -gamma, n_x)

    coef_theirs, land_theirs, row_total = backward(theirs, n_z, kern_theirs, dembed, feat, [], BF16)
    coef_mine, land_mine, row_total = backward(mine, n_z, kern_mine, dembed, feat, [row_total], F32)
    land_share = (land_mine + shift(land_theirs, "c", 1).astype(F32)).reshape(n_y, n_z, rows, width)
    land_share = collect(land_share, Y)

    own, first, second, opposite = feature_share(mine + theirs, n_z, [coef_mine, coef_theirs], feat_t, row_total, n_x, rank)
    landmark_grad = collect_at_once(land_share, "z")
    arrived = [partner(first, X, 0), partner(second, X, 1), shift(opposite, "x", 2)]
    feature_grad = (own + sum(share.astype(F32) for share in arrived)).T
    return (feature_grad, landmark_grad)


def solution(mesh):
    fine = Mesh(mesh.devices.reshape(4, 2, 2, 8, 2), ("x", "h", "l", "z", "c"))
    lm, tx = ("x", "h"), ("l", "z", "c")
    placed = (P(tx, None), P(lm + tx, None), P(lm + tx, None), P(tx, None))
    return jax.shard_map(
        per_device,
        mesh=fine,
        in_specs=placed,
        out_specs=(P(tx + lm, None), P(lm + tx, None)),
        check_vma=False,
    )
```

```python
import functools

import jax
import jax.numpy as jnp
from jax import lax
from jax.experimental import pallas as pl
from jax.experimental.pallas import tpu as pltpu
from jax.sharding import Mesh, PartitionSpec as P

X = ("x",)
Y = ("h", "l")
SHIFTS = (3, 2, 1)
F32 = jnp.float32
BF16 = jnp.bfloat16
LOG2E = 1.4426950408889634
WHOLE = pl.BlockSpec(memory_space=pltpu.VMEM)
PARAMS = pltpu.CompilerParams(vmem_limit_bytes=12 * 2**20)


def call(body, out_shape, *operands):
    return pl.pallas_call(
        body,
        out_shape=out_shape,
        in_specs=[WHOLE] * len(operands),
        out_specs=jax.tree.map(lambda _: WHOLE, out_shape),
        compiler_params=PARAMS,
    )(*operands)


def shaped(shape, kind):
    return jax.ShapeDtypeStruct(shape, kind)


def pack_body(quads, landmarks, whitening, out, land, white, sems):
    fetches = [pltpu.make_async_copy(landmarks, land, sems.at[0]), pltpu.make_async_copy(whitening, white, sems.at[1])]
    for fetch in fetches:
        fetch.start()
    for fetch in fetches:
        fetch.wait()
    rows = land.shape[0]
    part = rows // quads
    white32 = white[...].astype(F32)
    beside = jnp.concatenate([white32[q * part : (q + 1) * part] for q in range(quads)], axis=1).astype(BF16)
    for i in range(out.shape[0]):
        out[i, :rows] = land[...]
        out[i, rows:] = beside


def pack(landmarks, whitening, copies):
    rows, width = landmarks.shape
    quads = width // whitening.shape[1]
    return pl.pallas_call(
        functools.partial(pack_body, quads),
        out_shape=shaped((copies, rows + rows // quads, width), BF16),
        in_specs=[pl.BlockSpec(memory_space=pltpu.HBM)] * 2,
        scratch_shapes=[
            pltpu.VMEM(landmarks.shape, BF16),
            pltpu.VMEM(whitening.shape, BF16),
            pltpu.SemaphoreType.DMA((2,)),
        ],
        compiler_params=PARAMS,
    )(*[pltpu.with_memory_space_constraint(array, pltpu.HBM) for array in (landmarks, whitening)])


def unpack(block, rank):
    count, packed, width = block.shape
    quads = width // rank
    rows = packed * quads // (quads + 1)
    land = block[:, :rows].reshape(count * rows, width)
    white = block[:, rows:].astype(F32)
    white = jnp.stack([white[:, :, q * rank : (q + 1) * rank] for q in range(quads)], axis=1)
    return land, white.reshape(count * rows, rank).astype(BF16)


def pieces_of(stacks, members):
    for stack in stacks:
        for i in range(0, stack.shape[0], members):
            yield stack[i : i + members]


def prepare_body(parts, places, features, cot_t, feat, feat_t, sq_feat, cot):
    own = features.shape[0] // parts
    for i, place in enumerate(places()):
        start = pl.multiple_of(place * own, own)
        to = slice(i * own, (i + 1) * own)
        some = features[pl.ds(start, own), :]
        turned = some.T
        turned32 = turned.astype(F32)
        feat[to, :] = some
        feat_t[:, to] = turned
        sq_feat[:, to] = jnp.sum(turned32 * turned32, axis=0, keepdims=True)
        cot[:, to] = cot_t[:, pl.ds(start, own)].astype(F32)


def prepare(features, cot_t, parts, places, count):
    toks, width = features.shape
    toks = toks // parts * count
    rank = cot_t.shape[0]
    shapes = [shaped((toks, width), BF16), shaped((width, toks), BF16), shaped((1, toks), F32), shaped((rank, toks), F32)]
    return call(functools.partial(prepare_body, parts, places), shapes, features, cot_t)


def forward_body(count, members, rank, first, *refs):
    stacks, (feat_t, sq_feat), outs = refs[:count], refs[count : count + 2], refs[count + 2 + (not first) :]
    blocks = sum(stack.shape[0] for stack in stacks) // members
    kerns, embeds = outs[:blocks], outs[blocks:]
    width = feat_t.shape[0]
    scale = 4.0 / width * LOG2E
    bias = sq_feat[...] * (-scale)
    total = None if first else refs[count + 2][...]
    whites, values = [], []
    for block, kern in zip(pieces_of(stacks, members), kerns):
        land, white = unpack(block, rank)
        land32 = land.astype(F32)
        sq_land = jnp.sum(land32 * land32, axis=1, keepdims=True) * (-scale)
        cross = jnp.dot(land, feat_t[...], preferred_element_type=F32)
        value = jnp.exp2(cross * (2.0 * scale) + (bias + sq_land))
        kern[...] = value
        values.append(value.astype(BF16))
        whites.append(white.T)
    for white, value in zip(whites, values):
        part = jnp.dot(white, value, preferred_element_type=F32)
        total = part if total is None else total + part
    for embed in embeds:
        embed[...] = total.astype(embed.dtype)


def forward(blocks, members, feat_t, sq_feat, prior, last, rank):
    width, toks = feat_t.shape
    count = sum(block.shape[0] for block in blocks) // members
    rows = sum(block.size for block in blocks) // (width + rank) // count
    shapes = [shaped((rows, toks), F32)] * count + [shaped((rank, toks), kind) for kind in ([F32, BF16] if last else [F32])]
    outs = call(functools.partial(forward_body, len(blocks), members, rank, not prior), shapes, *blocks, feat_t, sq_feat, *prior)
    return outs[:count], outs[count:]


def moved(ref, place, places, bit):
    own = ref.shape[1] // places
    start = (place ^ bit) * own
    return ref[:, start : start + own].astype(F32)


def pair_sum_body(places, share, other, total, rounded):
    own = share.shape[1] // places
    for p in range(places):
        at = slice(p * own, (p + 1) * own)
        total[:, at] = share[:, at] + moved(other, p, places, 1)
    rounded[...] = total[...].astype(BF16)


def pair_sum(share, other, places):
    shapes = [shaped(share.shape, F32), shaped(share.shape, BF16)]
    return call(functools.partial(pair_sum_body, places), shapes, share, other)


def norm_body(factor, places, share, other, cot, out):
    own = cot.shape[1] // places
    for p in range(places):
        at = slice(p * own, (p + 1) * own)
        embed = share[:, at] + moved(other, p, places, 2)
        upstream = cot[:, at]
        scale = lax.rsqrt(jnp.mean(embed * embed, axis=0, keepdims=True) + 1e-06)
        normed = embed * scale
        grad = scale * (upstream - normed * jnp.mean(upstream * normed, axis=0, keepdims=True))
        out[:, at] = (factor * grad).astype(BF16)


def norm_backward(share, other, cot, factor, places):
    return call(functools.partial(norm_body, factor, places), shaped(cot.shape, BF16), share, other, cot)


def backward_body(count, members, rank, first, *refs):
    stacks, refs = refs[:count], refs[count:]
    blocks = sum(stack.shape[0] for stack in stacks) // members
    kerns, (dembed, feat) = refs[:blocks], refs[blocks : blocks + 2]
    coef, land_grad, row_total = refs[-3:]
    total = None if first else refs[blocks + 2][...]
    for i, block in enumerate(pieces_of(stacks, members)):
        land, white = unpack(block, rank)
        rows = land.shape[0]
        at = slice(i * rows, (i + 1) * rows)
        dkernel = jnp.dot(white, dembed[...], preferred_element_type=F32)
        value32 = dkernel * kerns[i][...]
        value = value32.astype(BF16)
        coef[at, :] = value
        part = jnp.sum(value32, axis=0, keepdims=True)
        total = part if total is None else total + part
        col_total = jnp.sum(value32, axis=1, keepdims=True)
        pulled = jnp.dot(value, feat[...], preferred_element_type=F32)
        land_grad[at, :] = (2.0 * (col_total * land.astype(F32) - pulled)).astype(land_grad.dtype)
    row_total[...] = total


def backward(blocks, members, kerns, dembed, feat, prior, kind):
    toks, width = feat.shape
    rows = sum(kern.shape[0] for kern in kerns)
    shapes = [shaped((rows, toks), BF16), shaped((rows, width), kind), shaped((1, toks), F32)]
    body = functools.partial(backward_body, len(blocks), members, dembed.shape[0], not prior)
    return call(body, shapes, *blocks, *kerns, dembed, feat, *prior)


def feature_body(count, members, coefs, rank, *refs):
    stacks, coef, (feat_t, row_total), outs = refs[:count], refs[count : count + coefs], refs[count + coefs : count + coefs + 2], refs[count + coefs + 2 :]
    each = sum(stack.shape[0] for stack in stacks) // members // coefs
    pulled = None
    for i, block in enumerate(pieces_of(stacks, members)):
        land, _ = unpack(block, rank)
        rows = land.shape[0]
        at = slice(i % each * rows, (i % each + 1) * rows)
        part = lax.dot_general(land, coef[i // each][at, :], (((0,), (0,)), ((), ())), preferred_element_type=F32)
        pulled = part if pulled is None else pulled + part
    grad = 2.0 * (row_total[...] * feat_t[...].astype(F32) - pulled)
    start = 0
    for out in outs:
        out[...] = grad[:, start : start + out.shape[1]].astype(out.dtype)
        start += out.shape[1]


def feature_share(blocks, members, coefs, feat_t, row_total, parts, rank):
    width, toks = feat_t.shape
    shapes = [shaped((width, toks // parts), kind) for kind in [F32] + [BF16] * (parts - 1)]
    body = functools.partial(feature_body, len(blocks), members, len(coefs), rank)
    return call(body, shapes, *blocks, *coefs, feat_t, row_total)


def shift(block, axes, step):
    size = lax.axis_size(axes)
    return lax.ppermute(block, axes, [(i, (i + step) % size) for i in range(size)])


def partner(block, ring, which):
    masks = (1, 3)
    perm = [(2 * i + c, 2 * (i ^ masks[which ^ c]) + c) for i in range(lax.axis_size(ring)) for c in range(2)]
    return lax.ppermute(block, ring + ("c",), perm)


def spread(block, axes):
    return [block] + [shift(block, axes, s) for s in SHIFTS]


def collect(pieces, axes):
    total = pieces[0]
    for s in (2, 1, 3):
        total = total + shift(pieces[SHIFTS.index(s) + 1].astype(BF16), axes, -s).astype(F32)
    return total


def collect_at_once(pieces, axes):
    return jnp.sum(lax.all_to_all(pieces.astype(BF16), axes, 0, 0, tiled=True).astype(F32), axis=0)


def per_device(features, landmarks, whitening, cotangent):
    toks, width = features.shape
    rank = whitening.shape[1]
    n_x, n_h, n_y, n_z = lax.axis_size("x"), lax.axis_size("h"), lax.axis_size(Y), lax.axis_size("z")
    rows = landmarks.shape[0]
    gamma = 4.0 / width

    def places():
        here, half, core = lax.axis_index("x"), lax.axis_index("h"), lax.axis_index("c")
        members = [here, here ^ (1 + 2 * core), here ^ (3 - 2 * core), here ^ 2]
        return [member * n_h + half for member in members]

    packed = lax.all_to_all(pack(landmarks, whitening, n_z), "z", 0, 0, tiled=True)
    feat, feat_t, sq_feat, cot = prepare(features, cotangent.T, n_x * n_h, places, n_x)
    packed, feat, feat_t, sq_feat, cot = lax.optimization_barrier((packed, feat, feat_t, sq_feat, cot))
    mine = spread(packed, Y)

    kern_own, embed = forward(mine[:1], n_z, feat_t, sq_feat, [], False, rank)
    *arrived, embed = lax.optimization_barrier((*mine[1:], *embed))
    mine = mine[:1] + arrived
    theirs = [shift(jnp.concatenate(mine, axis=0), "c", 1)]
    kern_mine, embed = forward(arrived, n_z, feat_t, sq_feat, [embed], False, rank)
    kern_theirs, (embed, share) = forward(theirs, n_z, feat_t, sq_feat, embed, True, rank)
    kern_mine = kern_own + kern_mine
    embed, share = pair_sum(embed, partner(share, X, 0), n_x)
    dembed = norm_backward(embed, partner(share, X, 1), cot, -gamma, n_x)

    coef_theirs, land_theirs, row_total = backward(theirs, n_z, kern_theirs, dembed, feat, [], BF16)
    coef_mine, land_mine, row_total = backward(mine, n_z, kern_mine, dembed, feat, [row_total], F32)
    land_share = (land_mine + shift(land_theirs, "c", 1).astype(F32)).reshape(n_y, n_z, rows, width)
    land_share = collect(land_share, Y)

    own, first, second, opposite = feature_share(mine + theirs, n_z, [coef_mine, coef_theirs], feat_t, row_total, n_x, rank)
    landmark_grad = collect_at_once(land_share, "z")
    arrived = [partner(first, X, 0), partner(second, X, 1), shift(opposite, "x", 2)]
    feature_grad = (own + sum(share.astype(F32) for share in arrived)).T
    return (feature_grad, landmark_grad)


def solution(mesh):
    fine = Mesh(mesh.devices.reshape(4, 2, 2, 8, 2), ("x", "h", "l", "z", "c"))
    lm, tx = ("x", "h"), ("l", "z", "c")
    placed = (P(tx, None), P(lm + tx, None), P(lm + tx, None), P(tx, None))
    return jax.shard_map(
        per_device,
        mesh=fine,
        in_specs=placed,
        out_specs=(P(tx + lm, None), P(lm + tx, None)),
        check_vma=False,
    )
```

```python
import functools

import jax
import jax.numpy as jnp
from jax import lax
from jax.experimental import pallas as pl
from jax.experimental.pallas import tpu as pltpu
from jax.sharding import Mesh, PartitionSpec as P

X = ("x",)
Y = ("h", "l")
SHIFTS = (3, 2, 1)
F32 = jnp.float32
BF16 = jnp.bfloat16
LOG2E = 1.4426950408889634
WHOLE = pl.BlockSpec(memory_space=pltpu.VMEM)
PARAMS = pltpu.CompilerParams(vmem_limit_bytes=12 * 2**20)


def call(body, out_shape, *operands):
    return pl.pallas_call(
        body,
        out_shape=out_shape,
        in_specs=[WHOLE] * len(operands),
        out_specs=jax.tree.map(lambda _: WHOLE, out_shape),
        compiler_params=PARAMS,
    )(*operands)


def shaped(shape, kind):
    return jax.ShapeDtypeStruct(shape, kind)


def pack_body(quads, landmarks, whitening, out, land, white, sems):
    fetches = [pltpu.make_async_copy(landmarks, land, sems.at[0]), pltpu.make_async_copy(whitening, white, sems.at[1])]
    for fetch in fetches:
        fetch.start()
    for fetch in fetches:
        fetch.wait()
    rows = land.shape[0]
    part = rows // quads
    white32 = white[...].astype(F32)
    beside = jnp.concatenate([white32[q * part : (q + 1) * part] for q in range(quads)], axis=1).astype(BF16)
    for i in range(out.shape[0]):
        out[i, :rows] = land[...]
        out[i, rows:] = beside


def pack(landmarks, whitening, copies):
    rows, width = landmarks.shape
    quads = width // whitening.shape[1]
    return pl.pallas_call(
        functools.partial(pack_body, quads),
        out_shape=shaped((copies, rows + rows // quads, width), BF16),
        in_specs=[pl.BlockSpec(memory_space=pltpu.HBM)] * 2,
        scratch_shapes=[
            pltpu.VMEM(landmarks.shape, BF16),
            pltpu.VMEM(whitening.shape, BF16),
            pltpu.SemaphoreType.DMA((2,)),
        ],
        compiler_params=PARAMS,
    )(*[pltpu.with_memory_space_constraint(array, pltpu.HBM) for array in (landmarks, whitening)])


def unpack(block, rank):
    count, packed, width = block.shape
    quads = width // rank
    rows = packed * quads // (quads + 1)
    land = block[:, :rows].reshape(count * rows, width)
    white = block[:, rows:].astype(F32)
    white = jnp.stack([white[:, :, q * rank : (q + 1) * rank] for q in range(quads)], axis=1)
    return land, white.reshape(count * rows, rank).astype(BF16)


def pieces_of(stacks, members):
    for stack in stacks:
        for i in range(0, stack.shape[0], members):
            yield stack[i : i + members]


def prepare_body(parts, places, features, cot_t, feat, feat_t, sq_feat, cot):
    own = features.shape[0] // parts
    for i, place in enumerate(places()):
        start = pl.multiple_of(place * own, own)
        to = slice(i * own, (i + 1) * own)
        some = features[pl.ds(start, own), :]
        turned = some.T
        turned32 = turned.astype(F32)
        feat[to, :] = some
        feat_t[:, to] = turned
        sq_feat[:, to] = jnp.sum(turned32 * turned32, axis=0, keepdims=True)
        cot[:, to] = cot_t[:, pl.ds(start, own)].astype(F32)


def prepare(features, cot_t, parts, places, count):
    toks, width = features.shape
    toks = toks // parts * count
    rank = cot_t.shape[0]
    shapes = [shaped((toks, width), BF16), shaped((width, toks), BF16), shaped((1, toks), F32), shaped((rank, toks), F32)]
    return call(functools.partial(prepare_body, parts, places), shapes, features, cot_t)


def forward_body(count, members, rank, first, *refs):
    stacks, (feat_t, sq_feat), outs = refs[:count], refs[count : count + 2], refs[count + 2 + (not first) :]
    blocks = sum(stack.shape[0] for stack in stacks) // members
    kerns, embeds = outs[:blocks], outs[blocks:]
    width = feat_t.shape[0]
    scale = 4.0 / width * LOG2E
    bias = sq_feat[...] * (-scale)
    total = None if first else refs[count + 2][...]
    whites, values = [], []
    for block, kern in zip(pieces_of(stacks, members), kerns):
        land, white = unpack(block, rank)
        land32 = land.astype(F32)
        sq_land = jnp.sum(land32 * land32, axis=1, keepdims=True) * (-scale)
        cross = jnp.dot(land, feat_t[...], preferred_element_type=F32)
        value = jnp.exp2(cross * (2.0 * scale) + (bias + sq_land))
        kern[...] = value
        values.append(value.astype(BF16))
        whites.append(white.T)
    for white, value in zip(whites, values):
        part = jnp.dot(white, value, preferred_element_type=F32)
        total = part if total is None else total + part
    for embed in embeds:
        embed[...] = total.astype(embed.dtype)


def forward(blocks, members, feat_t, sq_feat, prior, last, rank):
    width, toks = feat_t.shape
    count = sum(block.shape[0] for block in blocks) // members
    rows = sum(block.size for block in blocks) // (width + rank) // count
    shapes = [shaped((rows, toks), F32)] * count + [shaped((rank, toks), kind) for kind in ([F32, BF16] if last else [F32])]
    outs = call(functools.partial(forward_body, len(blocks), members, rank, not prior), shapes, *blocks, feat_t, sq_feat, *prior)
    return outs[:count], outs[count:]


def moved(ref, place, places, bit):
    own = ref.shape[1] // places
    start = (place ^ bit) * own
    return ref[:, start : start + own].astype(F32)


def pair_sum_body(places, share, other, total, rounded):
    own = share.shape[1] // places
    for p in range(places):
        at = slice(p * own, (p + 1) * own)
        total[:, at] = share[:, at] + moved(other, p, places, 1)
    rounded[...] = total[...].astype(BF16)


def pair_sum(share, other, places):
    shapes = [shaped(share.shape, F32), shaped(share.shape, BF16)]
    return call(functools.partial(pair_sum_body, places), shapes, share, other)


def norm_backward(factor, places, share, other, cot, out):
    own = cot.shape[1] // places
    for p in range(places):
        at = slice(p * own, (p + 1) * own)
        embed = share[:, at] + moved(other, p, places, 2)
        upstream = cot[:, at]
        scale = lax.rsqrt(jnp.mean(embed * embed, axis=0, keepdims=True) + 1e-06)
        normed = embed * scale
        grad = scale * (upstream - normed * jnp.mean(upstream * normed, axis=0, keepdims=True))
        out[:, at] = (factor * grad).astype(BF16)


def backward_body(count, members, rank, first, *refs):
    stacks, refs = refs[:count], refs[count:]
    blocks = sum(stack.shape[0] for stack in stacks) // members
    kerns, (dembed, feat) = refs[:blocks], refs[blocks : blocks + 2]
    coef, land_grad, row_total = refs[-3:]
    total = None if first else refs[blocks + 2][...]
    for i, block in enumerate(pieces_of(stacks, members)):
        land, white = unpack(block, rank)
        rows = land.shape[0]
        at = slice(i * rows, (i + 1) * rows)
        dkernel = jnp.dot(white, dembed[...], preferred_element_type=F32)
        value32 = dkernel * kerns[i][...]
        value = value32.astype(BF16)
        coef[at, :] = value
        part = jnp.sum(value32, axis=0, keepdims=True)
        total = part if total is None else total + part
        col_total = jnp.sum(value32, axis=1, keepdims=True)
        pulled = jnp.dot(value, feat[...], preferred_element_type=F32)
        land_grad[at, :] = (2.0 * (col_total * land.astype(F32) - pulled)).astype(land_grad.dtype)
    row_total[...] = total


def backward_first_body(count, members, rank, factor, places, *refs):
    *ins, share, other, cot, feat, coef, land_grad, row_total, dembed = refs
    norm_backward(factor, places, share, other, cot, dembed)
    backward_body(count, members, rank, True, *ins, dembed, feat, coef, land_grad, row_total)


def backward_shapes(kerns, feat, kind):
    toks, width = feat.shape
    rows = sum(kern.shape[0] for kern in kerns)
    return [shaped((rows, toks), BF16), shaped((rows, width), kind), shaped((1, toks), F32)]


def backward_first(blocks, members, kerns, shares, cot, feat, factor, places):
    rank = cot.shape[0]
    body = functools.partial(backward_first_body, len(blocks), members, rank, factor, places)
    shapes = backward_shapes(kerns, feat, BF16) + [shaped(cot.shape, BF16)]
    return call(body, shapes, *blocks, *kerns, *shares, cot, feat)


def backward(blocks, members, kerns, dembed, feat, prior):
    body = functools.partial(backward_body, len(blocks), members, dembed.shape[0], False)
    return call(body, backward_shapes(kerns, feat, F32), *blocks, *kerns, dembed, feat, prior)


def feature_body(count, members, coefs, rank, *refs):
    stacks, coef, (feat_t, row_total), outs = refs[:count], refs[count : count + coefs], refs[count + coefs : count + coefs + 2], refs[count + coefs + 2 :]
    each = sum(stack.shape[0] for stack in stacks) // members // coefs
    pulled = None
    for i, block in enumerate(pieces_of(stacks, members)):
        land, _ = unpack(block, rank)
        rows = land.shape[0]
        at = slice(i % each * rows, (i % each + 1) * rows)
        part = lax.dot_general(land, coef[i // each][at, :], (((0,), (0,)), ((), ())), preferred_element_type=F32)
        pulled = part if pulled is None else pulled + part
    grad = 2.0 * (row_total[...] * feat_t[...].astype(F32) - pulled)
    start = 0
    for out in outs:
        out[...] = grad[:, start : start + out.shape[1]].astype(out.dtype)
        start += out.shape[1]


def feature_share(blocks, members, coefs, feat_t, row_total, parts, rank):
    width, toks = feat_t.shape
    shapes = [shaped((width, toks // parts), kind) for kind in [F32] + [BF16] * (parts - 1)]
    body = functools.partial(feature_body, len(blocks), members, len(coefs), rank)
    return call(body, shapes, *blocks, *coefs, feat_t, row_total)


def shift(block, axes, step):
    size = lax.axis_size(axes)
    return lax.ppermute(block, axes, [(i, (i + step) % size) for i in range(size)])


def partner(block, ring, which):
    masks = (1, 3)
    perm = [(2 * i + c, 2 * (i ^ masks[which ^ c]) + c) for i in range(lax.axis_size(ring)) for c in range(2)]
    return lax.ppermute(block, ring + ("c",), perm)


def spread(block, axes):
    return [block] + [shift(block, axes, s) for s in SHIFTS]


def collect(pieces, axes):
    total = pieces[0]
    for s in (2, 1, 3):
        total = total + shift(pieces[SHIFTS.index(s) + 1].astype(BF16), axes, -s).astype(F32)
    return total


def collect_at_once(pieces, axes):
    return jnp.sum(lax.all_to_all(pieces.astype(BF16), axes, 0, 0, tiled=True).astype(F32), axis=0)


def per_device(features, landmarks, whitening, cotangent):
    toks, width = features.shape
    rank = whitening.shape[1]
    n_x, n_h, n_y, n_z = lax.axis_size("x"), lax.axis_size("h"), lax.axis_size(Y), lax.axis_size("z")
    rows = landmarks.shape[0]
    gamma = 4.0 / width

    def places():
        here, half, core = lax.axis_index("x"), lax.axis_index("h"), lax.axis_index("c")
        members = [here, here ^ (1 + 2 * core), here ^ (3 - 2 * core), here ^ 2]
        return [member * n_h + half for member in members]

    packed = lax.all_to_all(pack(landmarks, whitening, n_z), "z", 0, 0, tiled=True)
    feat, feat_t, sq_feat, cot = prepare(features, cotangent.T, n_x * n_h, places, n_x)
    packed, feat, feat_t, sq_feat, cot = lax.optimization_barrier((packed, feat, feat_t, sq_feat, cot))
    mine = spread(packed, Y)

    kern_own, embed = forward(mine[:1], n_z, feat_t, sq_feat, [], False, rank)
    *arrived, embed = lax.optimization_barrier((*mine[1:], *embed))
    mine = mine[:1] + arrived
    theirs = [shift(jnp.concatenate(mine, axis=0), "c", 1)]
    kern_mine, embed = forward(arrived, n_z, feat_t, sq_feat, [embed], False, rank)
    kern_theirs, (embed, share) = forward(theirs, n_z, feat_t, sq_feat, embed, True, rank)
    kern_mine = kern_own + kern_mine
    embed, share = pair_sum(embed, partner(share, X, 0), n_x)
    shares = [embed, partner(share, X, 1)]
    coef_theirs, land_theirs, row_total, dembed = backward_first(theirs, n_z, kern_theirs, shares, cot, feat, -gamma, n_x)
    coef_mine, land_mine, row_total = backward(mine, n_z, kern_mine, dembed, feat, row_total)
    land_share = (land_mine + shift(land_theirs, "c", 1).astype(F32)).reshape(n_y, n_z, rows, width)
    land_share = collect(land_share, Y)

    own, first, second, opposite = feature_share(mine + theirs, n_z, [coef_mine, coef_theirs], feat_t, row_total, n_x, rank)
    landmark_grad = collect_at_once(land_share, "z")
    arrived = [partner(first, X, 0), partner(second, X, 1), shift(opposite, "x", 2)]
    feature_grad = (own + sum(share.astype(F32) for share in arrived)).T
    return (feature_grad, landmark_grad)


def solution(mesh):
    fine = Mesh(mesh.devices.reshape(4, 2, 2, 8, 2), ("x", "h", "l", "z", "c"))
    lm, tx = ("x", "h"), ("l", "z", "c")
    placed = (P(tx, None), P(lm + tx, None), P(lm + tx, None), P(tx, None))
    return jax.shard_map(
        per_device,
        mesh=fine,
        in_specs=placed,
        out_specs=(P(tx + lm, None), P(lm + tx, None)),
        check_vma=False,
    )
```

```python
import functools

import jax
import jax.numpy as jnp
from jax import lax
from jax.experimental import pallas as pl
from jax.experimental.pallas import tpu as pltpu
from jax.sharding import Mesh, PartitionSpec as P

X = ("x",)
Y = ("h", "l")
SHIFTS = (3, 1, 2)
F32 = jnp.float32
BF16 = jnp.bfloat16
LOG2E = 1.4426950408889634
WHOLE = pl.BlockSpec(memory_space=pltpu.VMEM)
PARAMS = pltpu.CompilerParams(vmem_limit_bytes=12 * 2**20)


def call(body, out_shape, *operands):
    return pl.pallas_call(
        body,
        out_shape=out_shape,
        in_specs=[WHOLE] * len(operands),
        out_specs=jax.tree.map(lambda _: WHOLE, out_shape),
        compiler_params=PARAMS,
    )(*operands)


def shaped(shape, kind):
    return jax.ShapeDtypeStruct(shape, kind)


def pack_body(quads, landmarks, whitening, out, land, white, sems):
    fetches = [pltpu.make_async_copy(landmarks, land, sems.at[0]), pltpu.make_async_copy(whitening, white, sems.at[1])]
    for fetch in fetches:
        fetch.start()
    for fetch in fetches:
        fetch.wait()
    rows = land.shape[0]
    part = rows // quads
    white32 = white[...].astype(F32)
    beside = jnp.concatenate([white32[q * part : (q + 1) * part] for q in range(quads)], axis=1).astype(BF16)
    for i in range(out.shape[0]):
        out[i, :rows] = land[...]
        out[i, rows:] = beside


def pack(landmarks, whitening, copies):
    rows, width = landmarks.shape
    quads = width // whitening.shape[1]
    return pl.pallas_call(
        functools.partial(pack_body, quads),
        out_shape=shaped((copies, rows + rows // quads, width), BF16),
        in_specs=[pl.BlockSpec(memory_space=pltpu.HBM)] * 2,
        scratch_shapes=[
            pltpu.VMEM(landmarks.shape, BF16),
            pltpu.VMEM(whitening.shape, BF16),
            pltpu.SemaphoreType.DMA((2,)),
        ],
        compiler_params=PARAMS,
    )(*[pltpu.with_memory_space_constraint(array, pltpu.HBM) for array in (landmarks, whitening)])


def unpack(block, rank):
    count, packed, width = block.shape
    quads = width // rank
    rows = packed * quads // (quads + 1)
    land = block[:, :rows].reshape(count * rows, width)
    white = block[:, rows:].astype(F32)
    white = jnp.stack([white[:, :, q * rank : (q + 1) * rank] for q in range(quads)], axis=1)
    return land, white.reshape(count * rows, rank).astype(BF16)


def pieces_of(stacks, members):
    for stack in stacks:
        for i in range(0, stack.shape[0], members):
            yield stack[i : i + members]


def prepare_body(parts, places, features, cot_t, feat, feat_t, sq_feat, cot):
    own = features.shape[0] // parts
    for i, place in enumerate(places()):
        start = pl.multiple_of(place * own, own)
        to = slice(i * own, (i + 1) * own)
        some = features[pl.ds(start, own), :]
        turned = some.T
        turned32 = turned.astype(F32)
        feat[to, :] = some
        feat_t[:, to] = turned
        sq_feat[:, to] = jnp.sum(turned32 * turned32, axis=0, keepdims=True)
        cot[:, to] = cot_t[:, pl.ds(start, own)].astype(F32)


def prepare(features, cot_t, parts, places, count):
    toks, width = features.shape
    toks = toks // parts * count
    rank = cot_t.shape[0]
    shapes = [shaped((toks, width), BF16), shaped((width, toks), BF16), shaped((1, toks), F32), shaped((rank, toks), F32)]
    return call(functools.partial(prepare_body, parts, places), shapes, features, cot_t)


def forward_body(count, members, rank, first, *refs):
    stacks, (feat_t, sq_feat), outs = refs[:count], refs[count : count + 2], refs[count + 2 + (not first) :]
    blocks = sum(stack.shape[0] for stack in stacks) // members
    kerns, embeds = outs[:blocks], outs[blocks:]
    width = feat_t.shape[0]
    scale = 4.0 / width * LOG2E
    bias = sq_feat[...] * (-scale)
    total = None if first else refs[count + 2][...]
    whites, values = [], []
    for block, kern in zip(pieces_of(stacks, members), kerns):
        land, white = unpack(block, rank)
        land32 = land.astype(F32)
        sq_land = jnp.sum(land32 * land32, axis=1, keepdims=True) * (-scale)
        cross = jnp.dot(land, feat_t[...], preferred_element_type=F32)
        value = jnp.exp2(cross * (2.0 * scale) + (bias + sq_land))
        kern[...] = value
        values.append(value.astype(BF16))
        whites.append(white.T)
    for white, value in zip(whites, values):
        part = jnp.dot(white, value, preferred_element_type=F32)
        total = part if total is None else total + part
    for embed in embeds:
        embed[...] = total.astype(embed.dtype)


def forward(blocks, members, feat_t, sq_feat, prior, last, rank):
    width, toks = feat_t.shape
    count = sum(block.shape[0] for block in blocks) // members
    rows = sum(block.size for block in blocks) // (width + rank) // count
    shapes = [shaped((rows, toks), F32)] * count + [shaped((rank, toks), kind) for kind in ([F32, BF16] if last else [F32])]
    outs = call(functools.partial(forward_body, len(blocks), members, rank, not prior), shapes, *blocks, feat_t, sq_feat, *prior)
    return outs[:count], outs[count:]


def moved(ref, place, places, bit):
    own = ref.shape[1] // places
    start = (place ^ bit) * own
    return ref[:, start : start + own].astype(F32)


def pair_sum_body(places, share, other, total, rounded):
    own = share.shape[1] // places
    for p in range(places):
        at = slice(p * own, (p + 1) * own)
        total[:, at] = share[:, at] + moved(other, p, places, 1)
    rounded[...] = total[...].astype(BF16)


def pair_sum(share, other, places):
    shapes = [shaped(share.shape, F32), shaped(share.shape, BF16)]
    return call(functools.partial(pair_sum_body, places), shapes, share, other)


def norm_body(factor, places, share, other, cot, out):
    own = cot.shape[1] // places
    for p in range(places):
        at = slice(p * own, (p + 1) * own)
        embed = share[:, at] + moved(other, p, places, 2)
        upstream = cot[:, at]
        scale = lax.rsqrt(jnp.mean(embed * embed, axis=0, keepdims=True) + 1e-06)
        normed = embed * scale
        grad = scale * (upstream - normed * jnp.mean(upstream * normed, axis=0, keepdims=True))
        out[:, at] = (factor * grad).astype(BF16)


def norm_backward(share, other, cot, factor, places):
    return call(functools.partial(norm_body, factor, places), shaped(cot.shape, BF16), share, other, cot)


def backward_body(count, members, rank, first, *refs):
    stacks, refs = refs[:count], refs[count:]
    blocks = sum(stack.shape[0] for stack in stacks) // members
    kerns, (dembed, feat) = refs[:blocks], refs[blocks : blocks + 2]
    coef, land_grad, row_total = refs[-3:]
    total = None if first else refs[blocks + 2][...]
    for i, block in enumerate(pieces_of(stacks, members)):
        land, white = unpack(block, rank)
        rows = land.shape[0]
        at = slice(i * rows, (i + 1) * rows)
        dkernel = jnp.dot(white, dembed[...], preferred_element_type=F32)
        value32 = dkernel * kerns[i][...]
        value = value32.astype(BF16)
        coef[at, :] = value
        part = jnp.sum(value32, axis=0, keepdims=True)
        total = part if total is None else total + part
        col_total = jnp.sum(value32, axis=1, keepdims=True)
        pulled = jnp.dot(value, feat[...], preferred_element_type=F32)
        land_grad[at, :] = (2.0 * (col_total * land.astype(F32) - pulled)).astype(land_grad.dtype)
    row_total[...] = total


def backward(blocks, members, kerns, dembed, feat, prior, kind):
    toks, width = feat.shape
    rows = sum(kern.shape[0] for kern in kerns)
    shapes = [shaped((rows, toks), BF16), shaped((rows, width), kind), shaped((1, toks), F32)]
    body = functools.partial(backward_body, len(blocks), members, dembed.shape[0], not prior)
    return call(body, shapes, *blocks, *kerns, dembed, feat, *prior)


def feature_body(count, members, coefs, rank, *refs):
    stacks, coef, (feat_t, row_total), outs = refs[:count], refs[count : count + coefs], refs[count + coefs : count + coefs + 2], refs[count + coefs + 2 :]
    each = sum(stack.shape[0] for stack in stacks) // members // coefs
    pulled = None
    for i, block in enumerate(pieces_of(stacks, members)):
        land, _ = unpack(block, rank)
        rows = land.shape[0]
        at = slice(i % each * rows, (i % each + 1) * rows)
        part = lax.dot_general(land, coef[i // each][at, :], (((0,), (0,)), ((), ())), preferred_element_type=F32)
        pulled = part if pulled is None else pulled + part
    grad = 2.0 * (row_total[...] * feat_t[...].astype(F32) - pulled)
    start = 0
    for out in outs:
        out[...] = grad[:, start : start + out.shape[1]].astype(out.dtype)
        start += out.shape[1]


def feature_share(blocks, members, coefs, feat_t, row_total, parts, rank):
    width, toks = feat_t.shape
    shapes = [shaped((width, toks // parts), kind) for kind in [F32] + [BF16] * (parts - 1)]
    body = functools.partial(feature_body, len(blocks), members, len(coefs), rank)
    return call(body, shapes, *blocks, *coefs, feat_t, row_total)


def shift(block, axes, step):
    size = lax.axis_size(axes)
    return lax.ppermute(block, axes, [(i, (i + step) % size) for i in range(size)])


def partner(block, ring, which):
    masks = (1, 3)
    perm = [(2 * i + c, 2 * (i ^ masks[which ^ c]) + c) for i in range(lax.axis_size(ring)) for c in range(2)]
    return lax.ppermute(block, ring + ("c",), perm)


def spread(block, axes):
    return [block] + [shift(block, axes, s) for s in SHIFTS]


def collect(pieces, axes):
    total = pieces[0]
    for s in (2, 1, 3):
        total = total + shift(pieces[SHIFTS.index(s) + 1].astype(BF16), axes, -s).astype(F32)
    return total


def collect_at_once(pieces, axes):
    return jnp.sum(lax.all_to_all(pieces.astype(BF16), axes, 0, 0, tiled=True).astype(F32), axis=0)


def per_device(features, landmarks, whitening, cotangent):
    toks, width = features.shape
    rank = whitening.shape[1]
    n_x, n_h, n_y, n_z = lax.axis_size("x"), lax.axis_size("h"), lax.axis_size(Y), lax.axis_size("z")
    rows = landmarks.shape[0]
    gamma = 4.0 / width

    def places():
        here, half, core = lax.axis_index("x"), lax.axis_index("h"), lax.axis_index("c")
        members = [here, here ^ (1 + 2 * core), here ^ (3 - 2 * core), here ^ 2]
        return [member * n_h + half for member in members]

    packed = lax.all_to_all(pack(landmarks, whitening, n_z), "z", 0, 0, tiled=True)
    feat, feat_t, sq_feat, cot = prepare(features, cotangent.T, n_x * n_h, places, n_x)
    packed, feat, feat_t, sq_feat, cot = lax.optimization_barrier((packed, feat, feat_t, sq_feat, cot))
    mine = spread(packed, Y)

    kern_own, embed = forward(mine[:1], n_z, feat_t, sq_feat, [], False, rank)
    *arrived, embed = lax.optimization_barrier((*mine[1:], *embed))
    mine = mine[:1] + arrived
    theirs = [shift(jnp.concatenate(mine, axis=0), "c", 1)]
    kern_mine, embed = forward(arrived, n_z, feat_t, sq_feat, [embed], False, rank)
    kern_theirs, (embed, share) = forward(theirs, n_z, feat_t, sq_feat, embed, True, rank)
    kern_mine = kern_own + kern_mine
    embed, share = pair_sum(embed, partner(share, X, 0), n_x)
    dembed = norm_backward(embed, partner(share, X, 1), cot, -gamma, n_x)

    coef_theirs, land_theirs, row_total = backward(theirs, n_z, kern_theirs, dembed, feat, [], BF16)
    coef_mine, land_mine, row_total = backward(mine, n_z, kern_mine, dembed, feat, [row_total], F32)
    land_share = (land_mine + shift(land_theirs, "c", 1).astype(F32)).reshape(n_y, n_z, rows, width)
    land_share = collect(land_share, Y)

    own, first, second, opposite = feature_share(mine + theirs, n_z, [coef_mine, coef_theirs], feat_t, row_total, n_x, rank)
    landmark_grad = collect_at_once(land_share, "z")
    arrived = [partner(first, X, 0), partner(second, X, 1), shift(opposite, "x", 2)]
    feature_grad = (own + sum(share.astype(F32) for share in arrived)).T
    return (feature_grad, landmark_grad)


def solution(mesh):
    fine = Mesh(mesh.devices.reshape(4, 2, 2, 8, 2), ("x", "h", "l", "z", "c"))
    lm, tx = ("x", "h"), ("l", "z", "c")
    placed = (P(tx, None), P(lm + tx, None), P(lm + tx, None), P(tx, None))
    return jax.shard_map(
        per_device,
        mesh=fine,
        in_specs=placed,
        out_specs=(P(tx + lm, None), P(lm + tx, None)),
        check_vma=False,
    )
```
